32 devices in a mesh: replica: 8 (over z, y), shard: 4 (over x, core).
Axes of the slice: x: 2, y: 2, z: 4, core: 2. Of those that a mesh axis runs over, the one named last changes fastest.
Arguments:
- hidden_in: bfloat16 [4096, 1024], P(('replica', 'shard')), may hold values from -6 to 6
- out_grad: bfloat16 [4096, 1024], P(('replica', 'shard')), may hold values from -6 to 6
- lengths: int32 [32, 4], P(('replica', 'shard')), may hold values from 1 to 64, 128 in all within a row
- norm1_gain: bfloat16 [1024], P('shard'), may hold values from 0.099609375 to 1.8984375
- norm1_bias: bfloat16 [1024], P('shard'), may hold values from -3 to 3
- qkv_weight: bfloat16 [1024, 3072], P('shard'), may hold values from -0.1875 to 0.1875
- query_bias: bfloat16 [1024], P('shard'), may hold values from -3 to 3
- value_bias: bfloat16 [1024], P('shard'), may hold values from -3 to 3
- out_weight: bfloat16 [1024, 1024], P('shard'), may hold values from -0.75 to 0.75
- out_bias: bfloat16 [1024], P('shard'), may hold values from -3 to 3
- norm2_gain: bfloat16 [1024], P('shard'), may hold values from 0.099609375 to 1.8984375
- norm2_bias: bfloat16 [1024], P('shard'), may hold values from -3 to 3
- up_weight: bfloat16 [1024, 4096], P('shard'), may hold values from -0.1875 to 0.1875
- up_bias: bfloat16 [4096], P('shard'), may hold values from -3 to 3
- down_weight: bfloat16 [4096, 1024], P('shard'), may hold values from -0.125 to 0.125
- down_bias: bfloat16 [1024], P('shard'), may hold values from -3 to 3
Outputs:
- hidden_out: bfloat16 [4096, 1024], P(('replica', 'shard'))
- in_grad: bfloat16 [4096, 1024], P(('replica', 'shard'))
- norm1_gain_grad: float32 [1024], P('shard')
- norm1_bias_grad: float32 [1024], P('shard')
- qkv_weight_grad: float32 [1024, 3072], P('shard')
- query_bias_grad: float32 [1024], P('shard')
- value_bias_grad: float32 [1024], P('shard')
- out_weight_grad: float32 [1024, 1024], P('shard')
- out_bias_grad: float32 [1024], P('shard')
- norm2_gain_grad: float32 [1024], P('shard')
- norm2_bias_grad: float32 [1024], P('shard')
- up_weight_grad: float32 [1024, 4096], P('shard')
- up_bias_grad: float32 [4096], P('shard')
- down_weight_grad: float32 [4096, 1024], P('shard')
- down_bias_grad: float32 [1024], P('shard')
The draws below stay inside these ranges and needn't reach their ends.
Inputs may be any that keep to these rules, and one draw needn't show every extreme that they name: The 4 lengths of each device add up to 128, and the largest of all is 64.
All inputs are finite; a program needn't handle non-finite values.
Results may differ from the reference program's by a relative error of at most 0.018.
Values may be sent and summed in bfloat16 or wider, within the bound.
A program may use at most 192 MiB of HBM per device.

```python
import math
import jax
import jax.numpy as jnp
import numpy as np
from jax import lax

D = 1024
HEADS = 16
HEAD_DIM = 64
FF = 4096
TOK_DEV = 128
SEQS = 4
MOST = 64
TOKENS = 4096
N_REPLICA = 8
N_SHARD = 4


def block_levels(stream_key, shape, cuts, smallest, high):
    loudness = 1.0
    for position, parts in cuts:
        steps = jax.random.uniform(jax.random.fold_in(jax.random.fold_in(stream_key, 6), position), (parts,), jnp.float32, smallest / len(cuts), high / len(cuts))
        loudness = loudness * jnp.repeat(jnp.exp(steps), shape[position] // parts).reshape((-1,) + (1,) * (len(shape) - 1 - position))
    return loudness


def split_up(count, total, reach, slope):
    loads = [(1 << 20) // math.isqrt(grade ** slope) + 1 for grade in range(2, count + 1)]
    rest, counts = total - reach - (count - 1), [1] * (count - 1)
    while rest > 0:
        movable = [i for i in range(count - 1) if counts[i] < reach]
        mass, budget = sum([loads[i] for i in movable]), rest
        for i in movable:
            extra = min(reach - counts[i], max(1, budget * loads[i] // mass), rest)
            counts[i] = counts[i] + extra
            rest = rest - extra
    return np.array([reach] + counts)


def uneven_parts(key, amount, total, limit, lean):
    if amount == 2:
        one = jax.random.randint(key, (), max(1, total - limit), min(limit, total - 1) + 1)
        return jnp.stack([one, total - one])
    sizes = jnp.asarray(split_up(amount, total, limit, lean), jnp.int32)
    couples = (amount - 1) // 2
    giver, sink = sizes[1:1 + 2 * couples:2], sizes[2:2 + 2 * couples:2]
    room = jnp.minimum(giver - 1, limit - sink)
    shifted = jax.random.randint(jax.random.fold_in(key, 1), (couples,), 0, 1 << 20) % (room + 1)
    sizes = sizes.at[1:1 + 2 * couples:2].set(giver - shifted).at[2:2 + 2 * couples:2].set(sink + shifted)
    return sizes[jax.random.permutation(jax.random.fold_in(key, 2), amount)]


def normal_values(rng, dims, scale, reach, split=(), held_as=jnp.bfloat16):
    drawn = scale * jax.random.normal(rng, dims, jnp.float32)
    if split:
        drawn = drawn * block_levels(rng, dims, split, -0.22, 0.18)
    return jnp.clip(drawn, -reach, reach).astype(held_as)


def setup_inputs(seed: int = 0) -> dict:
    streams_of = jax.random.split(jax.random.key(seed), 17)
    hidden_in = normal_values(streams_of[0], (TOKENS, D), 1.0, 6.0, ((0, 32),))
    out_grad = normal_values(streams_of[1], (TOKENS, D), 1.0, 6.0, ((0, 32),))
    lengths = jax.vmap(lambda own: uneven_parts(own, SEQS, TOK_DEV, MOST, 2))(jax.random.split(streams_of[2], (N_REPLICA * N_SHARD))).reshape((N_REPLICA * N_SHARD, SEQS)).astype(jnp.int32)
    norm1_gain = jnp.clip(1.0 + 0.18 * jax.random.normal(streams_of[3], (D,), jnp.float32), 0.099609375, 1.8984375).astype(jnp.bfloat16)
    norm1_bias = normal_values(streams_of[4], (D,), 0.5, 3.0, ((0, 4),))
    qkv_weight = normal_values(streams_of[5], (D, 3 * D), D ** -0.5, 0.1875, ((0, 4),))
    query_bias = normal_values(streams_of[6], (D,), 0.5, 3.0, ((0, 4),))
    value_bias = normal_values(streams_of[7], (D,), 0.5, 3.0, ((0, 4),))
    out_weight = normal_values(streams_of[8], (D, D), (D // 16) ** -0.5, 0.75, ((0, 4),))
    out_bias = normal_values(streams_of[9], (D,), 0.5, 3.0, ((0, 4),))
    norm2_gain = jnp.clip(1.0 + 0.18 * jax.random.normal(streams_of[10], (D,), jnp.float32), 0.099609375, 1.8984375).astype(jnp.bfloat16)
    norm2_bias = normal_values(streams_of[11], (D,), 0.5, 3.0, ((0, 4),))
    up_weight = normal_values(streams_of[12], (D, FF), D ** -0.5, 0.1875, ((0, 4),))
    up_bias = normal_values(streams_of[13], (FF,), 0.5, 3.0, ((0, 4),))
    down_weight = normal_values(streams_of[14], (FF, D), (FF // 2) ** -0.5, 0.125, ((0, 4),))
    down_bias = normal_values(streams_of[15], (D,), 0.5, 3.0, ((0, 4),))
    return {"hidden_in": hidden_in, "out_grad": out_grad, "lengths": lengths, "norm1_gain": norm1_gain, "norm1_bias": norm1_bias, "qkv_weight": qkv_weight, "query_bias": query_bias, "value_bias": value_bias, "out_weight": out_weight, "out_bias": out_bias, "norm2_gain": norm2_gain, "norm2_bias": norm2_bias, "up_weight": up_weight, "up_bias": up_bias, "down_weight": down_weight, "down_bias": down_bias}


EPSILON = 1e-05
TANH_SCALE = math.sqrt(2.0 / math.pi)
CUBIC = 0.044715

def round_trip(source):
    return lax.optimization_barrier(source.astype(jnp.bfloat16)).astype(jnp.float32)

def product(left, right):
    return jnp.dot(left, right, preferred_element_type=jnp.float32)

def left_product(left, right):
    return jnp.dot(left.T, right, preferred_element_type=jnp.float32)

def right_product(left, right):
    return jnp.dot(left, right.T, preferred_element_type=jnp.float32)

def gelu_parts(pre_act):
    inner_arg = TANH_SCALE * (pre_act + CUBIC * pre_act * pre_act * pre_act)
    tangent = jnp.tanh(inner_arg)
    gelu_value = 0.5 * pre_act * (1.0 + tangent)
    gelu_slope = 0.5 * (1.0 + tangent) + 0.5 * pre_act * (1.0 - tangent * tangent) * TANH_SCALE * (1.0 + 3.0 * CUBIC * pre_act * pre_act)
    return (gelu_value, gelu_slope)

def layer_norm(inputs, gain_row, bias_row):
    average = lax.optimization_barrier(jnp.mean(inputs, axis=-1, keepdims=True))
    centred = inputs - average
    inv_std = lax.rsqrt(lax.optimization_barrier(jnp.mean(centred * centred, axis=-1, keepdims=True)) + EPSILON)
    normed = centred * inv_std
    return (normed * gain_row.astype(jnp.float32) + bias_row.astype(jnp.float32), normed, inv_std)

def norm_back(upstream, normed, inv_std, gain_row):
    scaled = upstream * gain_row.astype(jnp.float32)
    first_term = lax.optimization_barrier(jnp.mean(scaled, axis=-1, keepdims=True))
    second_term = lax.optimization_barrier(jnp.mean(scaled * normed, axis=-1, keepdims=True))
    input_grad = inv_std * (scaled - first_term - normed * second_term)
    return (input_grad, lax.optimization_barrier(jnp.sum(upstream * normed, axis=0)), lax.optimization_barrier(jnp.sum(upstream, axis=0)))

def seq_mask(lengths, row_count):
    seq_ends = jnp.cumsum(lengths, axis=-1).astype(jnp.int32)
    places = jnp.arange(row_count, dtype=jnp.int32)
    segment = lax.optimization_barrier(jnp.sum((places[None, :, None] >= seq_ends[:, None, :]).astype(jnp.int32), axis=-1))
    causal = places[None, :] <= places[:, None]
    return (segment[:, :, None] == segment[:, None, :]) & causal[None]

def split_heads(flat_rows, groups):
    return flat_rows.reshape(groups, -1, HEADS, HEAD_DIM).astype(jnp.float32)

def attend_forward(queries, key_rows, values, allowed):
    groups = allowed.shape[0]
    scale_factor = 1.0 / math.sqrt(HEAD_DIM)
    head_q = split_heads(queries, groups)
    head_k = split_heads(key_rows, groups)
    head_v = split_heads(values, groups)
    scores = jnp.einsum('gqhd,gkhd->ghqk', head_q, head_k) * scale_factor
    visible = allowed[:, None]
    row_total = lax.optimization_barrier(jnp.sum(jnp.where(visible, jnp.exp(scores), 0.0), axis=-1, keepdims=True))
    log_total = jnp.log(row_total)
    probs_round = round_trip(jnp.where(visible, jnp.exp(scores - log_total), 0.0))
    context = jnp.einsum('ghqk,gkhd->gqhd', probs_round, head_v)
    return (context.reshape(-1, HEADS * HEAD_DIM).astype(jnp.bfloat16), log_total)

def attend_backward(queries, key_rows, values, allowed, log_total, context_grad):
    groups = allowed.shape[0]
    scale_factor = 1.0 / math.sqrt(HEAD_DIM)
    head_q = split_heads(queries, groups)
    head_k = split_heads(key_rows, groups)
    head_v = split_heads(values, groups)
    head_g = split_heads(context_grad, groups)
    scores = jnp.einsum('gqhd,gkhd->ghqk', head_q, head_k) * scale_factor
    visible = allowed[:, None]
    exact_probs = jnp.where(visible, jnp.exp(scores - log_total), 0.0)
    probs_round = round_trip(exact_probs)
    prob_grad = jnp.einsum('gqhd,gkhd->ghqk', head_g, head_v)
    value_grad = jnp.einsum('ghqk,gqhd->gkhd', probs_round, head_g)
    row_delta = lax.optimization_barrier(jnp.sum(exact_probs * prob_grad, axis=-1, keepdims=True))
    score_grad = round_trip(exact_probs * (prob_grad - row_delta) * scale_factor)
    query_grad = jnp.einsum('ghqk,gkhd->gqhd', score_grad, head_k)
    key_grad = jnp.einsum('ghqk,gqhd->gkhd', score_grad, head_q)
    model_width = HEADS * HEAD_DIM
    return (query_grad.reshape(-1, model_width), key_grad.reshape(-1, model_width), value_grad.reshape(-1, model_width))

def whole_block(inputs, out_grad, allowed, weights_all):
    norm1_gain, norm1_bias, qkv_weight, query_bias, value_bias, out_weight, out_bias, norm2_gain, norm2_bias, up_weight, up_bias, down_weight, down_bias = weights_all
    model_width = inputs.shape[1]
    inputs_wide = inputs.astype(jnp.float32)
    first_out, normed_one, inv_one = layer_norm(inputs_wide, norm1_gain, norm1_bias)
    first_in = first_out.astype(jnp.bfloat16)
    projected = product(first_in, qkv_weight)
    queries = (projected[:, :model_width] + query_bias.astype(jnp.float32)).astype(jnp.bfloat16)
    key_rows = projected[:, model_width:2 * model_width].astype(jnp.bfloat16)
    values = (projected[:, 2 * model_width:] + value_bias.astype(jnp.float32)).astype(jnp.bfloat16)
    context, log_total = attend_forward(queries, key_rows, values, allowed)
    residual = inputs_wide + product(context, out_weight) + out_bias.astype(jnp.float32)
    second_out, normed_two, inv_two = layer_norm(residual, norm2_gain, norm2_bias)
    second_in = second_out.astype(jnp.bfloat16)
    pre_act = product(second_in, up_weight) + up_bias.astype(jnp.float32)
    activ_value, gelu_slope = gelu_parts(pre_act)
    activated = activ_value.astype(jnp.bfloat16)
    hidden_out = (residual + product(activated, down_weight) + down_bias.astype(jnp.float32)).astype(jnp.bfloat16)
    upstream = out_grad.astype(jnp.float32)
    down_wgrad = round_trip(left_product(activated, out_grad))
    down_bgrad = lax.optimization_barrier(jnp.sum(upstream, axis=0))
    pre_grad = right_product(out_grad, down_weight) * gelu_slope
    pre_round = pre_grad.astype(jnp.bfloat16)
    up_bgrad = lax.optimization_barrier(jnp.sum(pre_grad, axis=0))
    up_wgrad = round_trip(left_product(second_in, pre_round))
    second_grad = right_product(pre_round, up_weight)
    norm_two_in, gain2_grad, bias2_grad = norm_back(second_grad, normed_two, inv_two, norm2_gain)
    resid_grad = upstream + norm_two_in
    resid_round = resid_grad.astype(jnp.bfloat16)
    out_bgrad = lax.optimization_barrier(jnp.sum(resid_grad, axis=0))
    out_wgrad = round_trip(left_product(context, resid_round))
    context_grad = right_product(resid_round, out_weight).astype(jnp.bfloat16)
    query_grad, key_grad, value_grad = attend_backward(queries, key_rows, values, allowed, log_total, context_grad)
    query_bgrad = lax.optimization_barrier(jnp.sum(query_grad, axis=0))
    value_bgrad = lax.optimization_barrier(jnp.sum(value_grad, axis=0))
    qkv_grad = jnp.concatenate([query_grad, key_grad, value_grad], axis=1).astype(jnp.bfloat16)
    qkv_wgrad = round_trip(left_product(first_in, qkv_grad))
    first_grad = right_product(qkv_grad, qkv_weight)
    norm_one_in, gain1_grad, bias1_grad = norm_back(first_grad, normed_one, inv_one, norm1_gain)
    in_grad = (resid_grad + norm_one_in).astype(jnp.bfloat16)
    grads_all = (gain1_grad, bias1_grad, qkv_wgrad, query_bgrad, value_bgrad, out_wgrad, out_bgrad, gain2_grad, bias2_grad, up_wgrad, up_bgrad, down_wgrad, down_bgrad)
    return (hidden_out, in_grad, grads_all)

def reference(hidden_in, out_grad, lengths, norm1_gain, norm1_bias, qkv_weight, query_bias, value_bias, out_weight, out_bias, norm2_gain, norm2_bias, up_weight, up_bias, down_weight, down_bias):
    weights_all = (norm1_gain, norm1_bias, qkv_weight, query_bias, value_bias, out_weight, out_bias, norm2_gain, norm2_bias, up_weight, up_bias, down_weight, down_bias)
    device_count = lengths.shape[0]
    tok_count = hidden_in.shape[0] // device_count
    model_width = hidden_in.shape[1]
    inputs_all = hidden_in.reshape(device_count, tok_count, model_width)
    cotan_all = out_grad.reshape(device_count, tok_count, model_width)
    lengths_all = lengths.reshape(device_count, 1, lengths.shape[1])

    def advance(totals, element):
        inputs, cotan, lengths_now = element
        allowed = seq_mask(lengths_now, tok_count)
        hidden_out, in_grad, grads_all = whole_block(inputs, cotan, allowed, weights_all)
        return (tuple((total + grad for total, grad in zip(totals, grads_all))), (hidden_out, in_grad))
    initial = tuple((jnp.zeros(weight.shape, jnp.float32) for weight in weights_all))
    totals, (outs_all, grads_in) = lax.scan(advance, initial, (inputs_all, cotan_all, lengths_all))
    return (outs_all.reshape(hidden_in.shape), grads_in.reshape(hidden_in.shape), totals[0], totals[1], totals[2], totals[3], totals[4], totals[5], totals[6], totals[7], totals[8], totals[9], totals[10], totals[11], totals[12])
```

```python
import functools
import math

import jax
import jax.numpy as jnp
from jax import lax
from jax.experimental import pallas as pl
from jax.experimental.pallas import tpu as pltpu
from jax.sharding import PartitionSpec as P

HEADS = 16
HEAD_DIM = 64


EPSILON = 1e-05
TANH_SCALE = math.sqrt(2.0 / math.pi)
CUBIC = 0.044715


def product(left, right):
    return jnp.dot(left, right, preferred_element_type=jnp.float32)


def left_product(left, right):
    return lax.dot_general(
        left, right, (((0,), (0,)), ((), ())), preferred_element_type=jnp.float32
    )


def right_product(left, right):
    return lax.dot_general(
        left, right, (((1,), (1,)), ((), ())), preferred_element_type=jnp.float32
    )


def column_term(left, right):
    return left_product(left, right)


def gelu_parts(pre_act):
    inner_arg = TANH_SCALE * (pre_act + CUBIC * pre_act * pre_act * pre_act)
    tangent = jnp.tanh(inner_arg)
    gelu_value = 0.5 * pre_act * (1.0 + tangent)
    gelu_slope = 0.5 * (1.0 + tangent) + 0.5 * pre_act * (1.0 - tangent * tangent) * TANH_SCALE * (
        1.0 + 3.0 * CUBIC * pre_act * pre_act
    )
    return (gelu_value, gelu_slope)


def layer_norm(inputs, gain_row, bias_row):
    average = jnp.mean(inputs, axis=-1, keepdims=True)
    centred = inputs - average
    inv_std = lax.rsqrt(jnp.mean(centred * centred, axis=-1, keepdims=True) + EPSILON)
    normed = centred * inv_std
    return (normed * gain_row.astype(jnp.float32) + bias_row.astype(jnp.float32), normed, inv_std)


def norm_back(upstream, normed, inv_std, gain_row):
    scaled = upstream * gain_row.astype(jnp.float32)
    first_term = jnp.mean(scaled, axis=-1, keepdims=True)
    second_term = jnp.mean(scaled * normed, axis=-1, keepdims=True)
    input_grad = inv_std * (scaled - first_term - normed * second_term)
    return (input_grad, jnp.sum(upstream * normed, axis=0), jnp.sum(upstream, axis=0))


def seq_mask(lengths, row_count):
    seq_ends = jnp.cumsum(lengths, axis=-1)
    places = jnp.arange(row_count, dtype=jnp.int32)
    segment = jnp.sum((places[None, :, None] >= seq_ends[:, None, :]).astype(jnp.int32), axis=-1)
    causal = places[None, :] <= places[:, None]
    return (segment[:, :, None] == segment[:, None, :]) & causal[None]


def split_heads(flat_rows, groups):
    return flat_rows.reshape(groups, -1, flat_rows.shape[1] // HEAD_DIM, HEAD_DIM)


def attend_forward(queries, key_rows, values, allowed):
    groups = allowed.shape[0]
    scale_factor = 1.0 / math.sqrt(HEAD_DIM)
    head_q = split_heads(queries, groups)
    head_k = split_heads(key_rows, groups)
    head_v = split_heads(values, groups)
    scores = (
        jnp.einsum("gqhd,gkhd->ghqk", head_q, head_k, preferred_element_type=jnp.float32)
        * scale_factor
    )
    visible = allowed[:, None]
    row_total = jnp.sum(jnp.where(visible, jnp.exp(scores), 0.0), axis=-1, keepdims=True)
    log_total = jnp.log(row_total)
    probs_round = jnp.where(visible, jnp.exp(scores - log_total), 0.0).astype(jnp.bfloat16)
    context = jnp.einsum("ghqk,gkhd->gqhd", probs_round, head_v, preferred_element_type=jnp.float32)
    return (context.reshape(-1, queries.shape[1]).astype(jnp.bfloat16), log_total)


def attend_backward(queries, key_rows, values, allowed, log_total, context_grad):
    groups = allowed.shape[0]
    scale_factor = 1.0 / math.sqrt(HEAD_DIM)
    head_q = split_heads(queries, groups)
    head_k = split_heads(key_rows, groups)
    head_v = split_heads(values, groups)
    head_g = split_heads(context_grad, groups)
    scores = (
        jnp.einsum("gqhd,gkhd->ghqk", head_q, head_k, preferred_element_type=jnp.float32)
        * scale_factor
    )
    visible = allowed[:, None]
    exact_probs = jnp.where(visible, jnp.exp(scores - log_total), 0.0)
    probs_round = exact_probs.astype(jnp.bfloat16)
    prob_grad = jnp.einsum("gqhd,gkhd->ghqk", head_g, head_v, preferred_element_type=jnp.float32)
    value_grad = jnp.einsum(
        "ghqk,gqhd->gkhd", probs_round, head_g, preferred_element_type=jnp.float32
    )
    row_delta = jnp.sum(exact_probs * prob_grad, axis=-1, keepdims=True)
    score_grad = (exact_probs * (prob_grad - row_delta) * scale_factor).astype(jnp.bfloat16)
    query_grad = jnp.einsum(
        "ghqk,gkhd->gqhd", score_grad, head_k, preferred_element_type=jnp.float32
    )
    key_grad = jnp.einsum("ghqk,gqhd->gkhd", score_grad, head_q, preferred_element_type=jnp.float32)
    model_width = queries.shape[1]
    return (
        query_grad.reshape(-1, model_width),
        key_grad.reshape(-1, model_width),
        value_grad.reshape(-1, model_width),
    )


MESH = pl.DeviceIdType.MESH
VMEM_LIMIT = 60 * 1024 * 1024


def push(source, target, send_sem, recv_sem, device):
    return pltpu.make_async_remote_copy(
        src_ref=source,
        dst_ref=target,
        send_sem=send_sem,
        recv_sem=recv_sem,
        device_id=device,
        device_id_type=MESH,
    )


def greet(devices):
    barrier = pltpu.get_barrier_semaphore()
    for device in devices:
        pl.semaphore_signal(barrier, inc=1, device_id=device, device_id_type=MESH)
    pl.semaphore_wait(barrier, len(devices))


def group_peers(replica, me, size):
    return [(replica, lax.rem(me + k, size)) for k in range(1, size)]


class Spread:
    def __init__(self, blocks, replica, me, size, send, recv):
        core = lax.rem(me, 2)
        outer = me // 2
        half = size // 2
        self.partner = (replica, me + 1 - 2 * core)
        self.blocks, self.me, self.send, self.recv = blocks, me, send, recv
        self.size = size
        others = [lax.rem(outer + k, half) for k in range(1, half)]
        self.mates = [2 * j + core for j in others]
        self.far = [2 * j + 1 - core for j in others]
        self.replica = replica
        self.count = half

    def copy(self, k, block, device):
        return push(
            self.blocks.at[block], self.blocks.at[block], self.send.at[k], self.recv.at[block], device
        )

    def start(self):
        for k, mate in enumerate(self.mates):
            self.copy(k, self.me, (self.replica, mate)).start()
        self.copy(self.count, self.me, self.partner).start()

    def forward(self):
        for k, mate in enumerate(self.mates):
            self.copy(k, mate, self.partner).wait_recv()
            self.copy(self.count + 1 + k, mate, self.partner).start()

    def finish(self):
        for block in [self.partner[1]] + self.far:
            self.copy(0, block, self.partner).wait_recv()
        for k in range(len(self.mates)):
            self.copy(k, self.me, self.partner).wait_send()
            self.copy(self.count + 1 + k, self.me, self.partner).wait_send()
        self.copy(self.count, self.me, self.partner).wait_send()


def opening_kernel(size, hid_ref, grad_ref, par_ref, qkv_ref, up_ref,
                   hid_out, grad_out, par_out, qkv_out, up_out,
                   g_send, g_recv, w_send, w_recv, f_send, local_sem):
    replica = lax.axis_index("replica")
    me = lax.axis_index("shard")
    twin = replica + 1 - 2 * lax.rem(replica, 2)
    part = lax.rem(replica, 2)
    core = lax.rem(me, 2)
    outer = me // 2
    half = size // 2
    partner = me + 1 - 2 * core
    greet(group_peers(replica, me, size) + [(twin, me)])
    own = []
    for i, (src, dst) in enumerate(
        ((hid_ref, hid_out), (grad_ref, grad_out), (par_ref, par_out), (qkv_ref, qkv_out), (up_ref, up_out))
    ):
        if i < 3:
            own.append(pltpu.make_async_copy(src.at[0], dst.at[me], local_sem.at[i]))
        else:
            own.append(pltpu.make_async_copy(src.at[me], dst.at[me], local_sem.at[i]))
        own[-1].start()
    spreads = [
        Spread(out, replica, me, size, g_send.at[i], g_recv.at[i])
        for i, out in enumerate((hid_out, grad_out, par_out))
    ]
    own[0].wait()
    own[2].wait()
    spreads[2].start()
    spreads[0].start()
    remote = []
    for k in range(1, half):
        j = lax.rem(outer + k, half)
        remote += [2 * j + core, 2 * j + 1 - core]
    weights = ((qkv_ref, qkv_out), (up_ref, up_out))
    first = []
    for w, (src, dst) in enumerate(weights):
        for t, target in enumerate(remote):
            copy = push(
                src.at[target, part], dst.at[me, part],
                w_send.at[w, t], w_recv.at[w, me, part], (replica, target),
            )
            copy.start()
            first.append(copy)
        for h in range(2):
            copy = push(
                src.at[partner, h], dst.at[me, h],
                w_send.at[w, len(remote) + h], w_recv.at[w, me, h], (replica, partner),
            )
            copy.start()
            first.append(copy)
    own[1].wait()
    spreads[1].start()
    spreads[2].forward()
    spreads[0].forward()
    second = []
    for w, (src, dst) in enumerate(weights):
        for t, source in enumerate(remote):
            arrived = push(
                src.at[source, part], dst.at[source, part],
                w_send.at[w, t], w_recv.at[w, source, part], (replica, source),
            )
            arrived.wait_recv()
            copy = push(
                dst.at[source, part], dst.at[source, part],
                f_send.at[w, t], w_recv.at[w, source, part], (twin, me),
            )
            copy.start()
            second.append(copy)
    spreads[1].forward()
    for w, (src, dst) in enumerate(weights):
        for source in remote:
            push(
                dst.at[source, 1 - part], dst.at[source, 1 - part],
                f_send.at[w, 0], w_recv.at[w, source, 1 - part], (twin, me),
            ).wait_recv()
        for h in range(2):
            push(
                src.at[partner, h], dst.at[partner, h],
                w_send.at[w, 0], w_recv.at[w, partner, h], (replica, partner),
            ).wait_recv()
    for copy in first + second:
        copy.wait_send()
    own[3].wait()
    own[4].wait()
    for spread in spreads:
        spread.finish()


def vmem_specs(count):
    return [pl.BlockSpec(memory_space=pltpu.VMEM)] * count


def opening(size, hidden, upstream, params, qkv_parts, up_parts):
    dma = pltpu.SemaphoreType.DMA
    shape = lambda array: jax.ShapeDtypeStruct((size,) + array.shape[1:], array.dtype)
    arrays = (hidden[None], upstream[None], params[None], qkv_parts, up_parts)
    return pl.pallas_call(
        functools.partial(opening_kernel, size),
        out_shape=tuple(shape(a) for a in arrays),
        in_specs=vmem_specs(5),
        out_specs=tuple(vmem_specs(5)),
        scratch_shapes=[
            dma((3, size)), dma((3, size)), dma((2, size)), dma((2, size, 2)), dma((2, size)), dma((5,)),
        ],
        compiler_params=pltpu.CompilerParams(
            collective_id=0, has_side_effects=True, vmem_limit_bytes=VMEM_LIMIT
        ),
    )(*arrays)


def group_sum_kernel(size, gathers, *refs):
    n = len(gathers)
    half = size // 2
    ins, outs = refs[:n], refs[n : 2 * n]
    scratch = refs[2 * n :]
    replica = lax.axis_index("replica")
    me = lax.axis_index("shard")
    core = lax.rem(me, 2)
    outer = me // 2
    partner = (replica, me + 1 - 2 * core)
    greet(group_peers(replica, me, size))
    order = [lax.rem(outer + k, half) for k in range(1, half)] + [outer]
    work = []
    for i in range(n):
        near, summed, far, p_send, p_recv, x_send, x_recv, g_send, g_recv = scratch[9 * i : 9 * i + 9]
        for k, j in enumerate(order):
            push(
                ins[i].at[2 * j + 1 - core], near.at[j], p_send.at[k], p_recv.at[j], partner
            ).start()
    for i in range(n):
        near, summed, far, p_send, p_recv, x_send, x_recv, g_send, g_recv = scratch[9 * i : 9 * i + 9]
        for k, j in enumerate(order):
            push(ins[i].at[2 * j + 1 - core], near.at[j], p_send.at[k], p_recv.at[j], partner).wait_recv()
            if k < half - 1:
                block = ins[i][2 * j + core].astype(jnp.float32) + near[j].astype(jnp.float32)
                summed[k] = block.astype(jnp.bfloat16)
                push(
                    summed.at[k], far.at[outer], x_send.at[k], x_recv.at[outer], (replica, 2 * j + core)
                ).start()
    spreads = []
    for i in range(n):
        near, summed, far, p_send, p_recv, x_send, x_recv, g_send, g_recv = scratch[9 * i : 9 * i + 9]
        total = ins[i][me].astype(jnp.float32) + near[outer].astype(jnp.float32)
        for k, j in enumerate(order[:-1]):
            push(
                summed.at[k], far.at[j], x_send.at[k], x_recv.at[j], (replica, 2 * j + core)
            ).wait_recv()
            total = total + far[j].astype(jnp.float32)
        if gathers[i]:
            outs[i][me] = total.astype(outs[i].dtype)
            spread = Spread(outs[i], replica, me, size, g_send, g_recv)
            spread.start()
            spreads.append(spread)
        else:
            outs[i][...] = total.astype(outs[i].dtype)
    for spread in spreads:
        spread.forward()
    for spread in spreads:
        spread.finish()
    for i in range(n):
        near, summed, far, p_send, p_recv, x_send, x_recv, g_send, g_recv = scratch[9 * i : 9 * i + 9]
        for k, j in enumerate(order):
            push(ins[i].at[2 * j + 1 - core], near.at[j], p_send.at[k], p_recv.at[j], partner).wait_send()
            if k < half - 1:
                push(
                    summed.at[k], far.at[outer], x_send.at[k], x_recv.at[outer], (replica, 2 * j + core)
                ).wait_send()


def group_sum(size, partials, gathers, collective):
    dma = pltpu.SemaphoreType.DMA
    half = size // 2
    shapes, scratch, blocks = [], [], []
    for partial, gather in zip(partials, gathers):
        block = partial.reshape(size, -1, partial.shape[-1])
        blocks.append(block)
        if gather:
            shapes.append(jax.ShapeDtypeStruct(block.shape, jnp.bfloat16))
        else:
            shapes.append(jax.ShapeDtypeStruct(block.shape[1:], jnp.float32))
        for _ in range(3):
            scratch.append(pltpu.VMEM((half,) + block.shape[1:], jnp.bfloat16))
        scratch += [dma((half,)), dma((half,)), dma((half,)), dma((half,)), dma((size,)), dma((size,))]
    return pl.pallas_call(
        functools.partial(group_sum_kernel, size, gathers),
        out_shape=tuple(shapes),
        in_specs=vmem_specs(len(blocks)),
        out_specs=tuple(vmem_specs(len(blocks))),
        scratch_shapes=scratch,
        compiler_params=pltpu.CompilerParams(
            collective_id=collective, has_side_effects=True, vmem_limit_bytes=VMEM_LIMIT
        ),
    )(*blocks)


KEEP, SWAP, ADD = 0, 1, 2


def closing_kernel(size, ring, modes, *refs):
    n = len(modes)
    ins, outs, lands = refs[:n], refs[n : 2 * n], refs[2 * n : 3 * n]
    swaps = refs[3 * n : 4 * n]
    r_send, r_recv, a_send, a_recv, s_send, s_recv = refs[4 * n :]
    replica = lax.axis_index("replica")
    me = lax.axis_index("shard")
    side = lax.rem(replica, 2)
    depth = replica // 2
    place = (1 - side) * depth + side * (ring - 1 - depth)
    step = 1 - 2 * lax.rem(me, 2)

    def member(position):
        position = lax.rem(position + 2 * ring, ring)
        late = position // (ring // 2)
        return (1 - late) * 2 * position + late * (2 * (ring - 1 - position) + 1)

    after = (member(place + step), me)
    before = (member(place - step), me)
    chunk = lambda hops: lax.rem(place - step * hops + 2 * ring, ring)
    greet(group_peers(replica, me, size) + [after, before])

    def reduce_copy(i, k):
        source = ins[i].at[chunk(1)] if k == 0 else lands[i].at[k - 1]
        return push(source, lands[i].at[k], r_send.at[i, k], r_recv.at[i, k], after)

    for i in range(n):
        reduce_copy(i, 0).start()
    for k in range(ring - 1):
        for i in range(n):
            reduce_copy(i, k).wait_recv()
            mine = ins[i][chunk(k + 2)].astype(jnp.float32)
            total = (mine + lands[i][k].astype(jnp.float32)).astype(lands[i].dtype)
            lands[i][k] = total
            if k < ring - 2:
                reduce_copy(i, k + 1).start()
            elif modes[i] == KEEP:
                outs[i][place] = total

    def swap_copy(i, k, source):
        target = lax.rem(me + k, size)
        return push(
            lands[i].at[ring - 2, target], swaps[i].at[source],
            s_send.at[i, k], s_recv.at[i, source], (replica, target),
        )

    for i in range(n):
        if modes[i] != KEEP:
            for k in range(1, size):
                swap_copy(i, k, me).start()
            swaps[i][me] = lands[i][ring - 2, me]

    def gather_copy(i, k):
        return push(
            outs[i].at[chunk(k)], outs[i].at[chunk(k)], a_send.at[i, k], a_recv.at[i, k], after
        )

    def arrival(i, k):
        return push(
            outs[i].at[chunk(k + 1)], outs[i].at[chunk(k + 1)], a_send.at[i, k], a_recv.at[i, k], after
        )

    order = [i for i in range(n) if modes[i] == KEEP] + [i for i in range(n) if modes[i] != KEEP]
    for i in order:
        if modes[i] != KEEP:
            for k in range(1, size):
                swap_copy(i, size - k, lax.rem(me + k, size)).wait_recv()
            if modes[i] == SWAP:
                outs[i][place] = swaps[i][...]
            else:
                outs[i][place] = jnp.sum(swaps[i][...], axis=0)
        gather_copy(i, 0).start()
    for k in range(ring - 1):
        for i in order:
            arrival(i, k).wait_recv()
            if k < ring - 2:
                gather_copy(i, k + 1).start()
    for i in range(n):
        for k in range(ring - 1):
            reduce_copy(i, k).wait_send()
            gather_copy(i, k).wait_send()
        if modes[i] != KEEP:
            for k in range(1, size):
                swap_copy(i, k, me).wait_send()


def closing(size, ring, arrays, modes):
    dma = pltpu.SemaphoreType.DMA
    n = len(arrays)
    shapes, lands, swaps = [], [], []
    for array, mode in zip(arrays, modes):
        out = array.shape if mode != ADD else array.shape[:1] + array.shape[2:]
        shapes.append(jax.ShapeDtypeStruct(out, array.dtype))
        lands.append(pltpu.VMEM((ring - 1,) + array.shape[1:], array.dtype))
        swaps.append(
            pltpu.VMEM(array.shape[1:] if mode != KEEP else (8, 128), array.dtype)
        )
    return pl.pallas_call(
        functools.partial(closing_kernel, size, ring, modes),
        out_shape=tuple(shapes),
        in_specs=vmem_specs(n),
        out_specs=tuple(vmem_specs(n)),
        scratch_shapes=lands + swaps + [
            dma((n, ring)), dma((n, ring)), dma((n, ring)), dma((n, ring)), dma((n, size)), dma((n, size)),
        ],
        compiler_params=pltpu.CompilerParams(
            collective_id=5, has_side_effects=True, vmem_limit_bytes=VMEM_LIMIT
        ),
    )(*arrays)


def local(
    ring,
    size,
    hidden_in,
    out_grad,
    lengths,
    norm1_gain,
    norm1_bias,
    qkv_weight,
    query_bias,
    value_bias,
    out_weight,
    out_bias,
    norm2_gain,
    norm2_bias,
    up_weight,
    up_bias,
    down_weight,
    down_bias,
):
    me = lax.axis_index("shard")
    rows, width = hidden_in.shape
    band = width // size
    seqs = lengths.shape[1]
    lane_count = max(band, 128)
    wide = lambda vector: jnp.pad(vector, (0, lane_count - vector.shape[0]))
    params = jnp.stack(
        [
            wide(v)
            for v in (
                norm1_gain, norm1_bias, out_bias, norm2_gain, norm2_bias, down_bias,
                lengths[0].astype(jnp.bfloat16), norm1_gain,
            )
        ]
    )
    qkv_parts = qkv_weight.reshape(2, band // 2, 3, size, band).transpose(3, 0, 1, 2, 4)
    qkv_parts = qkv_parts.reshape(size, 2, band // 2, 3 * band)
    ff_band = up_weight.shape[1] // size
    up_parts = up_weight.reshape(2, band // 2, size, ff_band).transpose(2, 0, 1, 3)
    hidden_all, upstream_all, params_all, qkv_all, up_all = opening(
        size, hidden_in, out_grad, params, qkv_parts, up_parts
    )
    hidden_all = hidden_all.reshape(size * rows, width)
    grad_all = upstream_all.reshape(size * rows, width)
    qkv_cols = qkv_all.reshape(width, 3 * band)
    up_cols = up_all.reshape(width, ff_band)
    gain_one, bias_one, outb_full, gain_two, bias_two, downb_full = (
        params_all[:, i, :band].reshape(width) for i in range(6)
    )
    lengths_all = params_all[:, 6, :seqs].astype(jnp.int32)
    mine = lambda array: lax.dynamic_slice_in_dim(array, me * band, band, axis=array.ndim - 1)
    own_rows = lambda array: lax.dynamic_slice_in_dim(array, me * rows, rows, axis=0)

    allowed = seq_mask(lengths_all, rows)
    inputs_wide = hidden_all.astype(jnp.float32)
    first_out, normed_one, inv_one = layer_norm(inputs_wide, gain_one, bias_one)
    first_in = first_out.astype(jnp.bfloat16)
    projected = product(first_in, qkv_cols)
    queries = (projected[:, :band] + query_bias.astype(jnp.float32)).astype(jnp.bfloat16)
    key_rows = projected[:, band : 2 * band].astype(jnp.bfloat16)
    values = (projected[:, 2 * band :] + value_bias.astype(jnp.float32)).astype(jnp.bfloat16)
    context, log_total = attend_forward(queries, key_rows, values, allowed)
    (attended,) = group_sum(
        size, [product(context, out_weight).astype(jnp.bfloat16)], (True,), 1
    )
    residual = (
        inputs_wide
        + attended.reshape(size * rows, width).astype(jnp.float32)
        + outb_full.astype(jnp.float32)
    )
    second_out, normed_two, inv_two = layer_norm(residual, gain_two, bias_two)
    second_in = second_out.astype(jnp.bfloat16)
    pre_act = product(second_in, up_cols) + up_bias.astype(jnp.float32)
    activ_value, gelu_slope = gelu_parts(pre_act)
    activated = activ_value.astype(jnp.bfloat16)
    down_part = product(activated, down_weight).astype(jnp.bfloat16)
    upstream = grad_all.astype(jnp.float32)
    pre_grad = right_product(grad_all, down_weight) * gelu_slope
    pre_round = pre_grad.astype(jnp.bfloat16)
    second_part = right_product(pre_round, up_cols).astype(jnp.bfloat16)
    second_sum, down_sum = group_sum(size, [second_part, down_part], (True, False), 2)
    hidden_out = (own_rows(residual) + down_sum + downb_full.astype(jnp.float32)).astype(
        jnp.bfloat16
    )
    down_grad = column_term(activated, grad_all).astype(jnp.bfloat16)
    up_grad = column_term(second_in, pre_round).astype(jnp.bfloat16)
    second_grad = second_sum.reshape(size * rows, width).astype(jnp.float32)
    norm_two_in, gain2_grad, bias2_grad = norm_back(second_grad, normed_two, inv_two, gain_two)
    resid_grad = upstream + norm_two_in
    resid_round = resid_grad.astype(jnp.bfloat16)
    outw_grad = column_term(context, resid_round).astype(jnp.bfloat16)
    context_grad = right_product(resid_round, out_weight).astype(jnp.bfloat16)
    query_grad, key_grad, value_grad = attend_backward(
        queries, key_rows, values, allowed, log_total, context_grad
    )
    qkv_grad = jnp.concatenate([query_grad, key_grad, value_grad], axis=1).astype(jnp.bfloat16)
    first_part = right_product(qkv_grad, qkv_cols).astype(jnp.bfloat16)
    (first_grad,) = group_sum(size, [first_part], (False,), 3)
    qkvw_grad = column_term(first_in, qkv_grad).astype(jnp.bfloat16)
    norm_one_in, gain1_grad, bias1_grad = norm_back(
        first_grad, own_rows(normed_one), own_rows(inv_one), gain_one
    )
    in_grad = (own_rows(resid_grad) + norm_one_in).astype(jnp.bfloat16)

    owned = jnp.concatenate(
        [
            jnp.sum(query_grad, axis=0),
            jnp.sum(value_grad, axis=0),
            mine(jnp.sum(resid_grad, axis=0)),
            mine(gain2_grad),
            mine(bias2_grad),
            jnp.sum(pre_grad, axis=0),
            mine(jnp.sum(upstream, axis=0)),
        ]
    )
    here = (jnp.arange(size) == me)[:, None]
    small = jnp.concatenate(
        [
            gain1_grad.reshape(size, band),
            bias1_grad.reshape(size, band),
            jnp.where(here, owned[None], 0.0),
        ],
        axis=1,
    )
    count = small.shape[1]
    small = small.reshape(size, ring, 1, count // ring).transpose(1, 0, 2, 3)
    slab = band // ring
    by_owner = lambda array: array.reshape(size, ring, slab, array.shape[1]).transpose(1, 0, 2, 3)
    down_all, outw_all, up_total, qkv_total, small_all = closing(
        size,
        ring,
        [
            down_grad.reshape(ring, -1, width),
            outw_grad.reshape(ring, -1, width),
            by_owner(up_grad),
            by_owner(qkvw_grad),
            small,
        ],
        (KEEP, KEEP, SWAP, SWAP, ADD),
    )
    downw_total = down_all.reshape(down_weight.shape).astype(jnp.float32)
    outw_total = outw_all.reshape(out_weight.shape).astype(jnp.float32)
    upw_total = up_total.transpose(0, 2, 1, 3).reshape(up_weight.shape).astype(jnp.float32)
    qkvw_total = (
        qkv_total.reshape(ring, size, slab, 3, band)
        .transpose(0, 2, 3, 1, 4)
        .reshape(qkv_weight.shape)
        .astype(jnp.float32)
    )
    flat = small_all.reshape(count)
    pieces = []
    offset = 0
    for length in (band, band, band, band, band, band, band, ff_band, band):
        pieces.append(flat[offset : offset + length])
        offset += length
    gain1_t, bias1_t, qbias_t, vbias_t, outb_t, gain2_t, bias2_t, upb_t, downb_t = pieces
    return (
        hidden_out,
        in_grad,
        gain1_t,
        bias1_t,
        qkvw_total,
        qbias_t,
        vbias_t,
        outw_total,
        outb_t,
        gain2_t,
        bias2_t,
        upw_total,
        upb_t,
        downw_total,
        downb_t,
    )


def lanes(start, width):
    return pl.ds(pl.multiple_of(start, 128), width)


def entry_kernel(size, splits, hid_ref, grad_ref, par_ref, qkv_ref, up_ref,
                 hid_out, grad_out, par_out, qkv_out, up_out,
                 g_send, g_recv, w_send, w_recv, f_send, local_sem, own_sem):
    replica = lax.axis_index("replica")
    me = lax.axis_index("shard")
    twin = replica + 1 - 2 * lax.rem(replica, 2)
    part = lax.rem(replica, 2)
    core = lax.rem(me, 2)
    outer = me // 2
    half = size // 2
    partner = me + 1 - 2 * core
    weights = ((qkv_ref, qkv_out), (up_ref, up_out))
    own = []
    for i, (src, dst) in enumerate(((hid_ref, hid_out), (grad_ref, grad_out), (par_ref, par_out))):
        own.append(pltpu.make_async_copy(src.at[0], dst.at[me], local_sem.at[i]))
        own[-1].start()

    def views(w, owner, target, h):
        src, dst = weights[w]
        span = src.shape[2] // splits[w]
        wide = span // size
        for j in range(splits[w]):
            yield (
                j,
                src.at[h, :, lanes(j * span + target * wide, wide)],
                dst.at[owner, h, :, pl.ds(j * wide, wide)],
            )

    for w in range(2):
        for h in range(2):
            for j, source, target in views(w, me, me, h):
                own.append(pltpu.make_async_copy(source, target, own_sem.at[w, h, j]))
                own[-1].start()
    greet(group_peers(replica, me, size) + [(twin, me)])
    spreads = [
        Spread(out, replica, me, size, g_send.at[i], g_recv.at[i])
        for i, out in enumerate((hid_out, grad_out, par_out))
    ]
    own[0].wait()
    own[2].wait()
    spreads[2].start()
    spreads[0].start()
    remote = []
    for k in range(1, half):
        j = lax.rem(outer + k, half)
        remote += [2 * j + core, 2 * j + 1 - core]
    first = []
    for w in range(2):
        for t, target in enumerate(remote):
            for j, source, landing in views(w, me, target, part):
                copy = push(
                    source, landing, w_send.at[w, t, j], w_recv.at[w, me, part, j], (replica, target)
                )
                copy.start()
                first.append(copy)
        for h in range(2):
            for j, source, landing in views(w, me, partner, h):
                copy = push(
                    source, landing, w_send.at[w, len(remote) + h, j], w_recv.at[w, me, h, j],
                    (replica, partner),
                )
                copy.start()
                first.append(copy)
    own[1].wait()
    spreads[1].start()
    spreads[2].forward()
    spreads[0].forward()
    second = []
    for w in range(2):
        dst = weights[w][1]
        for t, source in enumerate(remote):
            for j, view, landing in views(w, source, me, part):
                push(
                    view, landing, w_send.at[w, t, j], w_recv.at[w, source, part, j], (replica, source)
                ).wait_recv()
            copy = push(
                dst.at[source, part], dst.at[source, part],
                f_send.at[w, t], w_recv.at[w, source, part, 0], (twin, me),
            )
            copy.start()
            second.append(copy)
    spreads[1].forward()
    for w in range(2):
        dst = weights[w][1]
        for source in remote:
            push(
                dst.at[source, 1 - part], dst.at[source, 1 - part],
                f_send.at[w, 0], w_recv.at[w, source, 1 - part, 0], (twin, me),
            ).wait_recv()
        for h in range(2):
            for j, view, landing in views(w, partner, me, h):
                push(
                    view, landing, w_send.at[w, 0, j], w_recv.at[w, partner, h, j], (replica, partner)
                ).wait_recv()
    for copy in first + second:
        copy.wait_send()
    for copy in own[3:]:
        copy.wait()
    for spread in spreads:
        spread.finish()


def entry(size, hidden, upstream, params, qkv_weight, up_weight):
    dma = pltpu.SemaphoreType.DMA
    band = qkv_weight.shape[0]
    shape = lambda array: jax.ShapeDtypeStruct((size,) + array.shape[1:], array.dtype)
    gathers = (hidden[None], upstream[None], params[None])
    weights = tuple(w.reshape(2, band // 2, w.shape[1]) for w in (qkv_weight, up_weight))
    outs = tuple(shape(a) for a in gathers) + tuple(
        jax.ShapeDtypeStruct((size, 2, band // 2, w.shape[2] // size), w.dtype) for w in weights
    )
    return pl.pallas_call(
        functools.partial(entry_kernel, size, (3, 1)),
        out_shape=outs,
        in_specs=[pl.BlockSpec(memory_space=pl.ANY)] * 5,
        out_specs=tuple(vmem_specs(5)),
        scratch_shapes=[
            dma((3, size)), dma((3, size)), dma((2, size, 3)), dma((2, size, 2, 3)), dma((2, size)),
            dma((3,)), dma((2, 2, 3)),
        ],
        compiler_params=pltpu.CompilerParams(
            collective_id=0, has_side_effects=True, vmem_limit_bytes=VMEM_LIMIT
        ),
    )(*gathers, *weights)


class Where:
    def __init__(self, size, ring):
        self.size, self.ring = size, ring
        self.replica = lax.axis_index("replica")
        self.me = lax.axis_index("shard")
        self.core = lax.rem(self.me, 2)
        self.outer = self.me // 2
        self.half = size // 2
        self.partner = (self.replica, self.me + 1 - 2 * self.core)
        self.order = [lax.rem(self.outer + k, self.half) for k in range(1, self.half)] + [self.outer]
        side = lax.rem(self.replica, 2)
        depth = self.replica // 2
        self.place = (1 - side) * depth + side * (ring - 1 - depth)
        self.step = 1 - 2 * self.core
        self.after = (self.member(self.place + self.step), self.me)
        self.before = (self.member(self.place - self.step), self.me)

    def member(self, position):
        ring = self.ring
        position = lax.rem(position + 2 * ring, ring)
        late = position // (ring // 2)
        return (1 - late) * 2 * position + late * (2 * (ring - 1 - position) + 1)

    def chunk(self, hops):
        return lax.rem(self.place - self.step * hops + 2 * self.ring, self.ring)


class Ring:
    def __init__(self, where, i, source, land, out, swap, sems, mode, pieces=1):
        self.where, self.source, self.land, self.out, self.swap = where, source, land, out, swap
        self.r_send, self.r_recv, self.a_send, self.a_recv, self.s_send, self.s_recv = (
            sem.at[i] for sem in sems
        )
        self.mode, self.pieces = mode, pieces
        self.last = where.ring - 2

    def block(self, position):
        return self.source.at[:, position] if self.mode == SWAP else self.source.at[position]

    def reduce_copy(self, k):
        source = self.block(self.where.chunk(1)) if k == 0 else self.land.at[k - 1]
        return push(source, self.land.at[k], self.r_send.at[k], self.r_recv.at[k], self.where.after)

    def swap_copy(self, k, source):
        where = self.where
        target = lax.rem(where.me + k, where.size)
        return push(
            self.land.at[self.last, target], self.swap.at[source],
            self.s_send.at[k], self.s_recv.at[source], (where.replica, target),
        )

    def gather_copy(self, k, hops):
        part = self.out.at[self.where.chunk(hops)]
        return push(part, part, self.a_send.at[k], self.a_recv.at[k], self.where.after)

    def start(self):
        self.reduce_copy(0).start()

    def reduce_step(self, k):
        where, land = self.where, self.land
        self.reduce_copy(k).wait_recv()
        position = where.chunk(k + 2)
        mine = self.source[:, position] if self.mode == SWAP else self.source[position]
        total = (mine.astype(jnp.float32) + land[k].astype(jnp.float32)).astype(land.dtype)
        land[k] = total
        if k < self.last:
            self.reduce_copy(k + 1).start()
        elif self.mode == KEEP:
            self.out[where.place] = total
            self.gather_copy(0, 0).start()
        else:
            for step in range(1, where.size):
                self.swap_copy(step, where.me).start()
            self.swap[where.me] = land[k, where.me]

    def turn(self):
        where = self.where
        if self.mode == KEEP:
            return
        for k in range(1, where.size):
            self.swap_copy(where.size - k, lax.rem(where.me + k, where.size)).wait_recv()
        if self.mode == ADD:
            self.out[where.place] = jnp.sum(self.swap[...], axis=0)
        else:
            wide = self.land.shape[-1] // self.pieces
            for s in range(where.size):
                for j in range(self.pieces):
                    start = (j * where.size + s) * wide
                    self.out[where.place, :, start : start + wide] = self.swap[
                        s, :, j * wide : (j + 1) * wide
                    ]
        self.gather_copy(0, 0).start()

    def gather_step(self, k):
        self.gather_copy(k, k + 1).wait_recv()
        if k < self.last:
            self.gather_copy(k + 1, k + 1).start()

    def stages(self):
        steps = [functools.partial(self.reduce_step, k) for k in range(self.last + 1)]
        if self.mode != KEEP:
            steps.append(self.turn)
        return steps + [functools.partial(self.gather_step, k) for k in range(self.last + 1)]

    def drain(self):
        for k in range(self.last + 1):
            self.reduce_copy(k).wait_send()
            self.gather_copy(k, k).wait_send()
        if self.mode != KEEP:
            for k in range(1, self.where.size):
                self.swap_copy(k, self.where.me).wait_send()


class GroupSum:
    def __init__(self, where, source, near, summed, far, sems):
        self.where, self.source, self.near, self.summed, self.far = where, source, near, summed, far
        self.p_send, self.p_recv, self.x_send, self.x_recv = sems

    def near_copy(self, k):
        j = self.where.order[k]
        return push(
            self.source.at[2 * j + 1 - self.where.core], self.near.at[j],
            self.p_send.at[k], self.p_recv.at[j], self.where.partner,
        )

    def far_copy(self, k, landing):
        where = self.where
        return push(
            self.summed.at[k], self.far.at[landing], self.x_send.at[k], self.x_recv.at[landing],
            (where.replica, 2 * where.order[k] + where.core),
        )

    def send(self, k):
        self.near_copy(k).start()

    def reduce(self, k):
        where = self.where
        j = where.order[k]
        self.near_copy(k).wait_recv()
        block = self.source[2 * j + where.core].astype(jnp.float32) + self.near[j].astype(jnp.float32)
        self.summed[k] = block.astype(jnp.bfloat16)
        self.far_copy(k, where.outer).start()

    def arrive(self):
        self.near_copy(self.where.half - 1).wait_recv()
        for k in range(self.where.half - 1):
            self.far_copy(k, self.where.order[k]).wait_recv()

    def tile(self, rows):
        where = self.where
        total = self.source[where.me, rows].astype(jnp.float32) + self.near[
            where.outer, rows
        ].astype(jnp.float32)
        for j in where.order[:-1]:
            total = total + self.far[j, rows].astype(jnp.float32)
        return total

    def drain(self):
        for k in range(self.where.half):
            self.near_copy(k).wait_send()
            if k < self.where.half - 1:
                self.far_copy(k, self.where.outer).wait_send()


TILE = 16


def tiles(count, body):
    @pl.loop(0, count // TILE)
    def _(t):
        body(pl.ds(pl.multiple_of(t * TILE, TILE), TILE))


def fold(value):
    return jnp.sum(value.reshape(TILE // 8, 8, value.shape[-1]), axis=0)


def row_stats(inputs):
    average = jnp.mean(inputs, axis=-1, keepdims=True)
    centred = inputs - average
    inv_std = lax.rsqrt(jnp.mean(centred * centred, axis=-1, keepdims=True) + EPSILON)
    return (centred * inv_std, inv_std)


def row_back(upstream, normed, inv_std, gain_row):
    scaled = upstream * gain_row
    first_term = jnp.mean(scaled, axis=-1, keepdims=True)
    second_term = jnp.mean(scaled * normed, axis=-1, keepdims=True)
    return inv_std * (scaled - first_term - normed * second_term)


def back_kernel(size, ring,
                second_ref, down_ref, dgrad_ref, ugrad_ref, resid_ref, grad_ref, hid_ref,
                q_ref, k_ref, v_ref, allow_ref, ctx_ref, outw_ref, first_ref, qkvw_ref,
                vec_ref, upb_ref,
                hidden_out, in_out, down_out, outw_out, up_out, qkv_out, small_out,
                near_a, summed_a, far_a, near_b, summed_b, far_b, near_c, summed_c, far_c,
                ssum, fpart, rgrad, rround, qkvg, outg, qkvwg, small, acc, bias,
                land_d, land_o, land_u, land_q, land_s, swap_u, swap_q, swap_s,
                p_send, p_recv, x_send, x_recv, g_send, g_recv,
                r_send, r_recv, a_send, a_recv, s_send, s_recv):
    where = Where(size, ring)
    me, replica = where.me, where.replica
    rows, width = hid_ref.shape
    band = q_ref.shape[2]
    slab = band // ring
    scale_factor = 1.0 / math.sqrt(HEAD_DIM)
    greet(group_peers(replica, me, size) + [where.after, where.before])
    sems = (r_send, r_recv, a_send, a_recv, s_send, s_recv)
    down_ring = Ring(where, 0, dgrad_ref, land_d, down_out, None, sems, KEEP)
    up_ring = Ring(where, 1, ugrad_ref, land_u, up_out, swap_u, sems, SWAP)
    outw_ring = Ring(where, 2, outg, land_o, outw_out, None, sems, KEEP)
    qkv_ring = Ring(where, 3, qkvwg, land_q, qkv_out, swap_q, sems, SWAP, 3)
    small_ring = Ring(where, 4, small, land_s, small_out, swap_s, sems, ADD)
    sums = []
    for i, buffers in enumerate(
        (
            (second_ref, near_a, summed_a, far_a),
            (down_ref, near_b, summed_b, far_b),
            (fpart, near_c, summed_c, far_c),
        )
    ):
        sums.append(
            GroupSum(where, *buffers, (p_send.at[i], p_recv.at[i], x_send.at[i], x_recv.at[i]))
        )
    second_sum, down_sum, first_sum = sums
    half = where.half

    for k in range(half):
        second_sum.send(k)
    up_ring.start()
    down_ring.start()
    early = []
    late_up, late_down = up_ring.stages(), down_ring.stages()
    while late_up or late_down:
        if late_up:
            early.append(late_up.pop(0))
        if late_down:
            early.append(late_down.pop(0))

    def serve(count):
        for _ in range(count):
            if early:
                early.pop(0)()

    for k in range(half - 1):
        second_sum.reduce(k)
    for k in range(half):
        down_sum.send(k)
    acc[...] = jnp.zeros_like(acc)
    bias[...] = jnp.zeros_like(bias)
    small[...] = jnp.zeros_like(small)
    second_sum.arrive()

    def second_total(part):
        ssum[me, part] = second_sum.tile(part).astype(jnp.bfloat16)

    tiles(rows, second_total)
    spread = Spread(ssum, replica, me, size, g_send, g_recv)
    spread.start()
    for k in range(half - 1):
        down_sum.reduce(k)
    serve(2)

    def norm_two(block):
        def body(part):
            normed, inv_std = row_stats(resid_ref[block, part])
            upper = ssum[block, part].astype(jnp.float32)
            total = grad_ref[block, part].astype(jnp.float32) + row_back(
                upper, normed, inv_std, vec_ref[1:2]
            )
            rgrad[block, part] = total
            rround[block, part] = total.astype(jnp.bfloat16)
            acc[0] += fold(upper * normed)
            acc[1] += fold(upper)
            acc[2] += fold(total)

        tiles(rows, body)

    norm_two(me)
    spread.forward()
    spread.finish()
    for k in range(1, size):
        norm_two(lax.rem(me + k, size))
    serve(2)

    lane = lax.broadcasted_iota(jnp.int32, (rows, 128), 1)
    sides = [(lane < HEAD_DIM), (lane >= HEAD_DIM)]
    masks = [side.astype(jnp.float32).astype(jnp.bfloat16) for side in sides]

    def block_back(block):
        context_grad = right_product(rround[block], outw_ref[...]).astype(jnp.bfloat16)
        visible = allow_ref[block] > 0.5
        for pair in range(band // 128):
            cut = slice(pair * 128, (pair + 1) * 128)
            query, key, value = q_ref[block, :, cut], k_ref[block, :, cut], v_ref[block, :, cut]
            upper = context_grad[:, cut]
            parts = []
            for mask in masks:
                scores = right_product(query * mask, key) * scale_factor
                total = jnp.sum(jnp.where(visible, jnp.exp(scores), 0.0), axis=-1, keepdims=True)
                probs = jnp.where(visible, jnp.exp(scores - jnp.log(total)), 0.0)
                prob_grad = right_product(upper * mask, value)
                delta = jnp.sum(probs * prob_grad, axis=-1, keepdims=True)
                score_grad = (probs * (prob_grad - delta) * scale_factor).astype(jnp.bfloat16)
                parts.append(
                    (
                        product(score_grad, key),
                        left_product(score_grad, query),
                        left_product(probs.astype(jnp.bfloat16), upper),
                    )
                )
            for j in range(3):
                grad = jnp.where(sides[0], parts[0][j], parts[1][j])
                start = j * band + pair * 128
                qkvg[block, :, start : start + 128] = grad.astype(jnp.bfloat16)
                if j != 1:
                    bias[:, start : start + 128] += jnp.sum(
                        grad.reshape(rows // 8, 8, 128), axis=0
                    )
        fpart[block] = right_product(qkvg[block], qkvw_ref[...]).astype(jnp.bfloat16)

    for k in range(half):
        block_back(2 * where.order[k] + 1 - where.core)
        first_sum.send(k)
        if k % 2 == 0:
            serve(1)
    for k in range(half):
        block_back(2 * where.order[k] + where.core)
        if k < half - 1:
            first_sum.reduce(k)
    serve(2)

    flat = lambda value: value.reshape(size * rows, value.shape[-1])

    @pl.loop(0, width // 256)
    def _(t):
        cut = lanes(t * 256, 256)
        grad = left_product(flat(ctx_ref[...]), flat(rround[:, :, cut]))
        outg[:, :, cut] = grad.astype(jnp.bfloat16).reshape(ring, slab, 256)

    outw_ring.start()

    @pl.loop(0, size)
    def _(t):
        grad = left_product(flat(first_ref[:, :, lanes(t * band, band)]), flat(qkvg[...]))
        qkvwg[t] = grad.astype(jnp.bfloat16).reshape(ring, slab, 3 * band)

    qkv_ring.start()
    serve(2)
    first_sum.arrive()

    def norm_one(part):
        normed, inv_std = row_stats(hid_ref[part].astype(jnp.float32))
        upper = first_sum.tile(part)
        total = rgrad[me, part] + row_back(upper, normed, inv_std, vec_ref[0:1])
        in_out[part] = total.astype(jnp.bfloat16)
        acc[3] += fold(upper * normed)
        acc[4] += fold(upper)

    tiles(rows, norm_one)
    down_sum.arrive()

    def finish_hidden(part):
        total = resid_ref[me, part] + down_sum.tile(part) + vec_ref[2:3]
        hidden_out[part] = total.astype(jnp.bfloat16)

    tiles(rows, finish_hidden)

    span = small.shape[3]

    def put(owner, start, row):
        for t in range(row.shape[1] // 128):
            position = start + t * 128
            small[position // span, owner, :, position % span : position % span + 128] = row[
                :, t * 128 : (t + 1) * 128
            ]

    for i in range(2):
        line = jnp.sum(acc[3 + i], axis=0, keepdims=True)
        for s in range(size):
            put(s, i * band, line[:, s * band : (s + 1) * band])
    start = 2 * band
    line = jnp.sum(bias[...], axis=0, keepdims=True)
    put(me, start, line[:, :band])
    put(me, start + band, line[:, 2 * band :])
    start += 2 * band
    for i in (2, 0, 1):
        put(me, start, jnp.sum(acc[i, :, lanes(me * band, band)], axis=0, keepdims=True))
        start += band
    put(me, start, upb_ref[...])
    start += upb_ref.shape[1]
    put(me, start, vec_ref[3:4, lanes(me * band, band)])
    small_ring.start()

    rest = [ring_.stages() for ring_ in (outw_ring, qkv_ring, small_ring)]
    while early or any(rest):
        serve(2)
        for stages in rest:
            if stages:
                stages.pop(0)()
    spread_free = (second_sum, down_sum, first_sum, down_ring, up_ring, outw_ring, qkv_ring, small_ring)
    for part in spread_free:
        part.drain()


def back(size, ring, arrays, small_count):
    dma = pltpu.SemaphoreType.DMA
    (second, down, dgrad, ugrad, resid, grads, hidden, q, k, v, allow, ctx, outw, first, qkvw, vec,
     upb) = arrays
    rows, width = hidden.shape
    band = q.shape[2]
    slab = band // ring
    half = size // 2
    ff_band = ugrad.shape[3]
    b16, f32 = jnp.bfloat16, jnp.float32
    vm = pltpu.VMEM
    scratch = [vm((half, rows, width), b16)] * 9
    scratch += [
        vm((size, rows, width), b16),
        vm((size, rows, width), b16),
        vm((size, rows, width), f32),
        vm((size, rows, width), b16),
        vm((size, rows, 3 * band), b16),
        vm((ring, slab, width), b16),
        vm((size, ring, slab, 3 * band), b16),
        vm((ring, size, 1, small_count // ring), f32),
        vm((5, 8, width), f32),
        vm((8, 3 * band), f32),
        vm((ring - 1,) + dgrad.shape[1:], b16),
        vm((ring - 1, slab, width), b16),
        vm((ring - 1, size, slab, ff_band), b16),
        vm((ring - 1, size, slab, 3 * band), b16),
        vm((ring - 1, size, 1, small_count // ring), f32),
        vm((size, slab, ff_band), b16),
        vm((size, slab, 3 * band), b16),
        vm((size, 1, small_count // ring), f32),
    ]
    scratch += [dma((3, half))] * 4 + [dma((size,))] * 2 + [dma((5, ring))] * 4 + [dma((5, size))] * 2
    shape = jax.ShapeDtypeStruct
    outs = (
        shape((rows, width), b16),
        shape((rows, width), b16),
        shape(dgrad.shape, b16),
        shape((ring, slab, width), b16),
        shape((ring, slab, size * ff_band), b16),
        shape((ring, slab, 3 * width), b16),
        shape((ring, 1, small_count // ring), f32),
    )
    return pl.pallas_call(
        functools.partial(back_kernel, size, ring),
        out_shape=outs,
        in_specs=vmem_specs(len(arrays)),
        out_specs=tuple(vmem_specs(len(outs))),
        scratch_shapes=scratch,
        compiler_params=pltpu.CompilerParams(
            collective_id=2, has_side_effects=True, vmem_limit_bytes=VMEM_LIMIT
        ),
    )(*arrays)


def fused(
    ring,
    size,
    hidden_in,
    out_grad,
    lengths,
    norm1_gain,
    norm1_bias,
    qkv_weight,
    query_bias,
    value_bias,
    out_weight,
    out_bias,
    norm2_gain,
    norm2_bias,
    up_weight,
    up_bias,
    down_weight,
    down_bias,
):
    rows, width = hidden_in.shape
    band = width // size
    seqs = lengths.shape[1]
    ff_band = up_weight.shape[1] // size
    params = jnp.concatenate(
        [
            norm1_gain, norm1_bias, out_bias, norm2_gain, norm2_bias, down_bias,
            jnp.pad(lengths[0].astype(jnp.bfloat16), (0, band - seqs)), norm1_gain,
        ]
    ).reshape(8, band)
    hidden_all, upstream_all, params_all, qkv_all, up_all = entry(
        size, hidden_in, out_grad, params, qkv_weight, up_weight
    )
    hidden_all = hidden_all.reshape(size * rows, width)
    grad_all = upstream_all.reshape(size * rows, width)
    qkv_cols = qkv_all.reshape(width, 3 * band)
    up_cols = up_all.reshape(width, ff_band)
    gain_one, bias_one, outb_full, gain_two, bias_two, downb_full = (
        params_all[:, i, :band].reshape(width) for i in range(6)
    )
    lengths_all = params_all[:, 6, :seqs].astype(jnp.int32)

    allowed = seq_mask(lengths_all, rows)
    inputs_wide = hidden_all.astype(jnp.float32)
    first_out, _, _ = layer_norm(inputs_wide, gain_one, bias_one)
    first_in = first_out.astype(jnp.bfloat16)
    projected = product(first_in, qkv_cols)
    queries = (projected[:, :band] + query_bias.astype(jnp.float32)).astype(jnp.bfloat16)
    key_rows = projected[:, band : 2 * band].astype(jnp.bfloat16)
    values = (projected[:, 2 * band :] + value_bias.astype(jnp.float32)).astype(jnp.bfloat16)
    by_block = lambda array: array.reshape(size, rows, array.shape[-1])
    allow = allowed.astype(jnp.float32)
    context = attend(by_block(queries), by_block(key_rows), by_block(values), allow)
    (attended,) = group_sum(
        size,
        [product(context.reshape(size * rows, band), out_weight).astype(jnp.bfloat16)],
        (True,),
        1,
    )
    residual = (
        inputs_wide
        + attended.reshape(size * rows, width).astype(jnp.float32)
        + outb_full.astype(jnp.float32)
    )
    second_out, _, _ = layer_norm(residual, gain_two, bias_two)
    second_in = second_out.astype(jnp.bfloat16)
    pre_act = product(second_in, up_cols) + up_bias.astype(jnp.float32)
    activ_value, gelu_slope = gelu_parts(pre_act)
    activated = activ_value.astype(jnp.bfloat16)
    down_part = product(activated, down_weight).astype(jnp.bfloat16)
    upstream = grad_all.astype(jnp.float32)
    pre_grad = right_product(grad_all, down_weight) * gelu_slope
    pre_round = pre_grad.astype(jnp.bfloat16)
    second_part = right_product(pre_round, up_cols).astype(jnp.bfloat16)
    down_grad = column_term(activated, grad_all).astype(jnp.bfloat16)
    up_grad = column_term(second_in, pre_round).astype(jnp.bfloat16)
    vectors = jnp.stack(
        [
            gain_one.astype(jnp.float32),
            gain_two.astype(jnp.float32),
            downb_full.astype(jnp.float32),
            jnp.sum(upstream, axis=0),
        ]
    )
    slab = band // ring
    lengths_out = (band, band, band, band, band, band, band, ff_band, band)
    hidden_out, in_grad, down_all, outw_all, up_total, qkv_total, small_all = back(
        size,
        ring,
        (
            by_block(second_part),
            by_block(down_part),
            down_grad.reshape(ring, -1, width),
            up_grad.reshape(size, ring, slab, ff_band),
            by_block(residual),
            by_block(grad_all),
            hidden_in,
            by_block(queries),
            by_block(key_rows),
            by_block(values),
            allow,
            context,
            out_weight,
            by_block(first_in),
            qkv_cols,
            vectors,
            jnp.sum(pre_grad, axis=0)[None],
        ),
        sum(lengths_out),
    )
    final = lambda array, like: array.reshape(like.shape).astype(jnp.float32)
    flat = small_all.reshape(-1)
    pieces = []
    offset = 0
    for length in lengths_out:
        pieces.append(flat[offset : offset + length])
        offset += length
    gain1_t, bias1_t, qbias_t, vbias_t, outb_t, gain2_t, bias2_t, upb_t, downb_t = pieces
    return (
        hidden_out,
        in_grad,
        gain1_t,
        bias1_t,
        final(qkv_total, qkv_weight),
        qbias_t,
        vbias_t,
        final(outw_all, out_weight),
        outb_t,
        gain2_t,
        bias2_t,
        final(up_total, up_weight),
        upb_t,
        final(down_all, down_weight),
        downb_t,
    )


def attend_kernel(q_ref, k_ref, v_ref, allow_ref, ctx_ref):
    rows, band = q_ref.shape[1:]
    lane = lax.broadcasted_iota(jnp.int32, (rows, 128), 1)
    sides = [(lane < HEAD_DIM), (lane >= HEAD_DIM)]
    masks = [side.astype(jnp.float32).astype(jnp.bfloat16) for side in sides]

    @pl.loop(0, q_ref.shape[0])
    def _(block):
        visible = allow_ref[block] > 0.5
        for pair in range(band // 128):
            cut = slice(pair * 128, (pair + 1) * 128)
            query, key, value = q_ref[block, :, cut], k_ref[block, :, cut], v_ref[block, :, cut]
            parts = []
            for mask in masks:
                scores = right_product(query * mask, key) * (1.0 / math.sqrt(HEAD_DIM))
                total = jnp.sum(jnp.where(visible, jnp.exp(scores), 0.0), axis=-1, keepdims=True)
                probs = jnp.where(visible, jnp.exp(scores - jnp.log(total)), 0.0)
                parts.append(product(probs.astype(jnp.bfloat16), value))
            ctx_ref[block, :, cut] = jnp.where(sides[0], parts[0], parts[1]).astype(jnp.bfloat16)


def attend(queries, key_rows, values, allow):
    return pl.pallas_call(
        attend_kernel,
        out_shape=jax.ShapeDtypeStruct(queries.shape, queries.dtype),
        in_specs=vmem_specs(4),
        out_specs=vmem_specs(1)[0],
    )(queries, key_rows, values, allow)


def choose(ring, size, hidden_in, *rest):
    rows, width = hidden_in.shape
    band = width // size
    aligned = width % size == 0 and band % 256 == 0 and band % (16 * ring) == 0
    body = fused if aligned and rows % 128 == 0 and size % 2 == 0 and ring % 2 == 0 else local
    return body(ring, size, hidden_in, *rest)


def solution(mesh):
    in_specs = (
        P(("replica", "shard"), None),
        P(("replica", "shard"), None),
        P(("replica", "shard"), None),
        P("shard"),
        P("shard"),
        P("shard", None),
        P("shard"),
        P("shard"),
        P("shard", None),
        P("shard"),
        P("shard"),
        P("shard"),
        P("shard", None),
        P("shard"),
        P("shard", None),
        P("shard"),
    )
    out_specs = (
        P(("replica", "shard"), None),
        P(("replica", "shard"), None),
        P("shard"),
        P("shard"),
        P("shard", None),
        P("shard"),
        P("shard"),
        P("shard", None),
        P("shard"),
        P("shard"),
        P("shard"),
        P("shard", None),
        P("shard"),
        P("shard", None),
        P("shard"),
    )
    body = functools.partial(choose, mesh.shape["replica"], mesh.shape["shard"])
    return jax.shard_map(body, mesh=mesh, in_specs=in_specs, out_specs=out_specs, check_vma=False)
```

```python
import functools
import math

import jax
import jax.numpy as jnp
from jax import lax
from jax.experimental import pallas as pl
from jax.experimental.pallas import tpu as pltpu
from jax.sharding import PartitionSpec as P

HEADS = 16
HEAD_DIM = 64


EPSILON = 1e-05
TANH_SCALE = math.sqrt(2.0 / math.pi)
CUBIC = 0.044715


def product(left, right):
    return jnp.dot(left, right, preferred_element_type=jnp.float32)


def left_product(left, right):
    return lax.dot_general(
        left, right, (((0,), (0,)), ((), ())), preferred_element_type=jnp.float32
    )


def right_product(left, right):
    return lax.dot_general(
        left, right, (((1,), (1,)), ((), ())), preferred_element_type=jnp.float32
    )


def column_term(left, right):
    return left_product(left, right)


def gelu_parts(pre_act):
    inner_arg = TANH_SCALE * (pre_act + CUBIC * pre_act * pre_act * pre_act)
    tangent = jnp.tanh(inner_arg)
    gelu_value = 0.5 * pre_act * (1.0 + tangent)
    gelu_slope = 0.5 * (1.0 + tangent) + 0.5 * pre_act * (1.0 - tangent * tangent) * TANH_SCALE * (
        1.0 + 3.0 * CUBIC * pre_act * pre_act
    )
    return (gelu_value, gelu_slope)


def layer_norm(inputs, gain_row, bias_row):
    average = jnp.mean(inputs, axis=-1, keepdims=True)
    centred = inputs - average
    inv_std = lax.rsqrt(jnp.mean(centred * centred, axis=-1, keepdims=True) + EPSILON)
    normed = centred * inv_std
    return (normed * gain_row.astype(jnp.float32) + bias_row.astype(jnp.float32), normed, inv_std)


def norm_back(upstream, normed, inv_std, gain_row):
    scaled = upstream * gain_row.astype(jnp.float32)
    first_term = jnp.mean(scaled, axis=-1, keepdims=True)
    second_term = jnp.mean(scaled * normed, axis=-1, keepdims=True)
    input_grad = inv_std * (scaled - first_term - normed * second_term)
    return (input_grad, jnp.sum(upstream * normed, axis=0), jnp.sum(upstream, axis=0))


def seq_mask(lengths, row_count):
    seq_ends = jnp.cumsum(lengths, axis=-1)
    places = jnp.arange(row_count, dtype=jnp.int32)
    segment = jnp.sum((places[None, :, None] >= seq_ends[:, None, :]).astype(jnp.int32), axis=-1)
    causal = places[None, :] <= places[:, None]
    return (segment[:, :, None] == segment[:, None, :]) & causal[None]


def split_heads(flat_rows, groups):
    return flat_rows.reshape(groups, -1, flat_rows.shape[1] // HEAD_DIM, HEAD_DIM)


def attend_forward(queries, key_rows, values, allowed):
    groups = allowed.shape[0]
    scale_factor = 1.0 / math.sqrt(HEAD_DIM)
    head_q = split_heads(queries, groups)
    head_k = split_heads(key_rows, groups)
    head_v = split_heads(values, groups)
    scores = (
        jnp.einsum("gqhd,gkhd->ghqk", head_q, head_k, preferred_element_type=jnp.float32)
        * scale_factor
    )
    visible = allowed[:, None]
    row_total = jnp.sum(jnp.where(visible, jnp.exp(scores), 0.0), axis=-1, keepdims=True)
    log_total = jnp.log(row_total)
    probs_round = jnp.where(visible, jnp.exp(scores - log_total), 0.0).astype(jnp.bfloat16)
    context = jnp.einsum("ghqk,gkhd->gqhd", probs_round, head_v, preferred_element_type=jnp.float32)
    return (context.reshape(-1, queries.shape[1]).astype(jnp.bfloat16), log_total)


def attend_backward(queries, key_rows, values, allowed, log_total, context_grad):
    groups = allowed.shape[0]
    scale_factor = 1.0 / math.sqrt(HEAD_DIM)
    head_q = split_heads(queries, groups)
    head_k = split_heads(key_rows, groups)
    head_v = split_heads(values, groups)
    head_g = split_heads(context_grad, groups)
    scores = (
        jnp.einsum("gqhd,gkhd->ghqk", head_q, head_k, preferred_element_type=jnp.float32)
        * scale_factor
    )
    visible = allowed[:, None]
    exact_probs = jnp.where(visible, jnp.exp(scores - log_total), 0.0)
    probs_round = exact_probs.astype(jnp.bfloat16)
    prob_grad = jnp.einsum("gqhd,gkhd->ghqk", head_g, head_v, preferred_element_type=jnp.float32)
    value_grad = jnp.einsum(
        "ghqk,gqhd->gkhd", probs_round, head_g, preferred_element_type=jnp.float32
    )
    row_delta = jnp.sum(exact_probs * prob_grad, axis=-1, keepdims=True)
    score_grad = (exact_probs * (prob_grad - row_delta) * scale_factor).astype(jnp.bfloat16)
    query_grad = jnp.einsum(
        "ghqk,gkhd->gqhd", score_grad, head_k, preferred_element_type=jnp.float32
    )
    key_grad = jnp.einsum("ghqk,gqhd->gkhd", score_grad, head_q, preferred_element_type=jnp.float32)
    model_width = queries.shape[1]
    return (
        query_grad.reshape(-1, model_width),
        key_grad.reshape(-1, model_width),
        value_grad.reshape(-1, model_width),
    )


MESH = pl.DeviceIdType.MESH
VMEM_LIMIT = 60 * 1024 * 1024


def push(source, target, send_sem, recv_sem, device):
    return pltpu.make_async_remote_copy(
        src_ref=source,
        dst_ref=target,
        send_sem=send_sem,
        recv_sem=recv_sem,
        device_id=device,
        device_id_type=MESH,
    )


def greet(devices):
    barrier = pltpu.get_barrier_semaphore()
    for device in devices:
        pl.semaphore_signal(barrier, inc=1, device_id=device, device_id_type=MESH)
    pl.semaphore_wait(barrier, len(devices))


def group_peers(replica, me, size):
    return [(replica, lax.rem(me + k, size)) for k in range(1, size)]


class Spread:
    def __init__(self, blocks, replica, me, size, send, recv):
        core = lax.rem(me, 2)
        outer = me // 2
        half = size // 2
        self.partner = (replica, me + 1 - 2 * core)
        self.blocks, self.me, self.send, self.recv = blocks, me, send, recv
        self.size = size
        others = [lax.rem(outer + k, half) for k in range(1, half)]
        self.mates = [2 * j + core for j in others]
        self.far = [2 * j + 1 - core for j in others]
        self.replica = replica
        self.count = half

    def copy(self, k, block, device):
        return push(
            self.blocks.at[block], self.blocks.at[block], self.send.at[k], self.recv.at[block], device
        )

    def start(self):
        for k, mate in enumerate(self.mates):
            self.copy(k, self.me, (self.replica, mate)).start()
        self.copy(self.count, self.me, self.partner).start()

    def forward(self):
        for k, mate in enumerate(self.mates):
            self.copy(k, mate, self.partner).wait_recv()
            self.copy(self.count + 1 + k, mate, self.partner).start()

    def finish(self):
        for block in [self.partner[1]] + self.far:
            self.copy(0, block, self.partner).wait_recv()
        for k in range(len(self.mates)):
            self.copy(k, self.me, self.partner).wait_send()
            self.copy(self.count + 1 + k, self.me, self.partner).wait_send()
        self.copy(self.count, self.me, self.partner).wait_send()


def opening_kernel(size, hid_ref, grad_ref, par_ref, qkv_ref, up_ref,
                   hid_out, grad_out, par_out, qkv_out, up_out,
                   g_send, g_recv, w_send, w_recv, f_send, local_sem):
    replica = lax.axis_index("replica")
    me = lax.axis_index("shard")
    twin = replica + 1 - 2 * lax.rem(replica, 2)
    part = lax.rem(replica, 2)
    core = lax.rem(me, 2)
    outer = me // 2
    half = size // 2
    partner = me + 1 - 2 * core
    greet(group_peers(replica, me, size) + [(twin, me)])
    own = []
    for i, (src, dst) in enumerate(
        ((hid_ref, hid_out), (grad_ref, grad_out), (par_ref, par_out), (qkv_ref, qkv_out), (up_ref, up_out))
    ):
        if i < 3:
            own.append(pltpu.make_async_copy(src.at[0], dst.at[me], local_sem.at[i]))
        else:
            own.append(pltpu.make_async_copy(src.at[me], dst.at[me], local_sem.at[i]))
        own[-1].start()
    spreads = [
        Spread(out, replica, me, size, g_send.at[i], g_recv.at[i])
        for i, out in enumerate((hid_out, grad_out, par_out))
    ]
    own[0].wait()
    own[2].wait()
    spreads[2].start()
    spreads[0].start()
    remote = []
    for k in range(1, half):
        j = lax.rem(outer + k, half)
        remote += [2 * j + core, 2 * j + 1 - core]
    weights = ((qkv_ref, qkv_out), (up_ref, up_out))
    first = []
    for w, (src, dst) in enumerate(weights):
        for t, target in enumerate(remote):
            copy = push(
                src.at[target, part], dst.at[me, part],
                w_send.at[w, t], w_recv.at[w, me, part], (replica, target),
            )
            copy.start()
            first.append(copy)
        for h in range(2):
            copy = push(
                src.at[partner, h], dst.at[me, h],
                w_send.at[w, len(remote) + h], w_recv.at[w, me, h], (replica, partner),
            )
            copy.start()
            first.append(copy)
    own[1].wait()
    spreads[1].start()
    spreads[2].forward()
    spreads[0].forward()
    second = []
    for w, (src, dst) in enumerate(weights):
        for t, source in enumerate(remote):
            arrived = push(
                src.at[source, part], dst.at[source, part],
                w_send.at[w, t], w_recv.at[w, source, part], (replica, source),
            )
            arrived.wait_recv()
            copy = push(
                dst.at[source, part], dst.at[source, part],
                f_send.at[w, t], w_recv.at[w, source, part], (twin, me),
            )
            copy.start()
            second.append(copy)
    spreads[1].forward()
    for w, (src, dst) in enumerate(weights):
        for source in remote:
            push(
                dst.at[source, 1 - part], dst.at[source, 1 - part],
                f_send.at[w, 0], w_recv.at[w, source, 1 - part], (twin, me),
            ).wait_recv()
        for h in range(2):
            push(
                src.at[partner, h], dst.at[partner, h],
                w_send.at[w, 0], w_recv.at[w, partner, h], (replica, partner),
            ).wait_recv()
    for copy in first + second:
        copy.wait_send()
    own[3].wait()
    own[4].wait()
    for spread in spreads:
        spread.finish()


def vmem_specs(count):
    return [pl.BlockSpec(memory_space=pltpu.VMEM)] * count


def opening(size, hidden, upstream, params, qkv_parts, up_parts):
    dma = pltpu.SemaphoreType.DMA
    shape = lambda array: jax.ShapeDtypeStruct((size,) + array.shape[1:], array.dtype)
    arrays = (hidden[None], upstream[None], params[None], qkv_parts, up_parts)
    return pl.pallas_call(
        functools.partial(opening_kernel, size),
        out_shape=tuple(shape(a) for a in arrays),
        in_specs=vmem_specs(5),
        out_specs=tuple(vmem_specs(5)),
        scratch_shapes=[
            dma((3, size)), dma((3, size)), dma((2, size)), dma((2, size, 2)), dma((2, size)), dma((5,)),
        ],
        compiler_params=pltpu.CompilerParams(
            collective_id=0, has_side_effects=True, vmem_limit_bytes=VMEM_LIMIT
        ),
    )(*arrays)


def group_sum_kernel(size, gathers, *refs):
    n = len(gathers)
    half = size // 2
    ins, outs = refs[:n], refs[n : 2 * n]
    scratch = refs[2 * n :]
    replica = lax.axis_index("replica")
    me = lax.axis_index("shard")
    core = lax.rem(me, 2)
    outer = me // 2
    partner = (replica, me + 1 - 2 * core)
    greet(group_peers(replica, me, size))
    order = [lax.rem(outer + k, half) for k in range(1, half)] + [outer]
    work = []
    for i in range(n):
        near, summed, far, p_send, p_recv, x_send, x_recv, g_send, g_recv = scratch[9 * i : 9 * i + 9]
        for k, j in enumerate(order):
            push(
                ins[i].at[2 * j + 1 - core], near.at[j], p_send.at[k], p_recv.at[j], partner
            ).start()
    for i in range(n):
        near, summed, far, p_send, p_recv, x_send, x_recv, g_send, g_recv = scratch[9 * i : 9 * i + 9]
        for k, j in enumerate(order):
            push(ins[i].at[2 * j + 1 - core], near.at[j], p_send.at[k], p_recv.at[j], partner).wait_recv()
            if k < half - 1:
                block = ins[i][2 * j + core].astype(jnp.float32) + near[j].astype(jnp.float32)
                summed[k] = block.astype(jnp.bfloat16)
                push(
                    summed.at[k], far.at[outer], x_send.at[k], x_recv.at[outer], (replica, 2 * j + core)
                ).start()
    spreads = []
    for i in range(n):
        near, summed, far, p_send, p_recv, x_send, x_recv, g_send, g_recv = scratch[9 * i : 9 * i + 9]
        total = ins[i][me].astype(jnp.float32) + near[outer].astype(jnp.float32)
        for k, j in enumerate(order[:-1]):
            push(
                summed.at[k], far.at[j], x_send.at[k], x_recv.at[j], (replica, 2 * j + core)
            ).wait_recv()
            total = total + far[j].astype(jnp.float32)
        if gathers[i]:
            outs[i][me] = total.astype(outs[i].dtype)
            spread = Spread(outs[i], replica, me, size, g_send, g_recv)
            spread.start()
            spreads.append(spread)
        else:
            outs[i][...] = total.astype(outs[i].dtype)
    for spread in spreads:
        spread.forward()
    for spread in spreads:
        spread.finish()
    for i in range(n):
        near, summed, far, p_send, p_recv, x_send, x_recv, g_send, g_recv = scratch[9 * i : 9 * i + 9]
        for k, j in enumerate(order):
            push(ins[i].at[2 * j + 1 - core], near.at[j], p_send.at[k], p_recv.at[j], partner).wait_send()
            if k < half - 1:
                push(
                    summed.at[k], far.at[outer], x_send.at[k], x_recv.at[outer], (replica, 2 * j + core)
                ).wait_send()


def group_sum(size, partials, gathers, collective):
    dma = pltpu.SemaphoreType.DMA
    half = size // 2
    shapes, scratch, blocks = [], [], []
    for partial, gather in zip(partials, gathers):
        block = partial.reshape(size, -1, partial.shape[-1])
        blocks.append(block)
        if gather:
            shapes.append(jax.ShapeDtypeStruct(block.shape, jnp.bfloat16))
        else:
            shapes.append(jax.ShapeDtypeStruct(block.shape[1:], jnp.float32))
        for _ in range(3):
            scratch.append(pltpu.VMEM((half,) + block.shape[1:], jnp.bfloat16))
        scratch += [dma((half,)), dma((half,)), dma((half,)), dma((half,)), dma((size,)), dma((size,))]
    return pl.pallas_call(
        functools.partial(group_sum_kernel, size, gathers),
        out_shape=tuple(shapes),
        in_specs=vmem_specs(len(blocks)),
        out_specs=tuple(vmem_specs(len(blocks))),
        scratch_shapes=scratch,
        compiler_params=pltpu.CompilerParams(
            collective_id=collective, has_side_effects=True, vmem_limit_bytes=VMEM_LIMIT
        ),
    )(*blocks)


KEEP, SWAP, ADD = 0, 1, 2


def closing_kernel(size, ring, modes, *refs):
    n = len(modes)
    ins, outs, lands = refs[:n], refs[n : 2 * n], refs[2 * n : 3 * n]
    swaps = refs[3 * n : 4 * n]
    r_send, r_recv, a_send, a_recv, s_send, s_recv = refs[4 * n :]
    replica = lax.axis_index("replica")
    me = lax.axis_index("shard")
    side = lax.rem(replica, 2)
    depth = replica // 2
    place = (1 - side) * depth + side * (ring - 1 - depth)
    step = 1 - 2 * lax.rem(me, 2)

    def member(position):
        position = lax.rem(position + 2 * ring, ring)
        late = position // (ring // 2)
        return (1 - late) * 2 * position + late * (2 * (ring - 1 - position) + 1)

    after = (member(place + step), me)
    before = (member(place - step), me)
    chunk = lambda hops: lax.rem(place - step * hops + 2 * ring, ring)
    greet(group_peers(replica, me, size) + [after, before])

    def reduce_copy(i, k):
        source = ins[i].at[chunk(1)] if k == 0 else lands[i].at[k - 1]
        return push(source, lands[i].at[k], r_send.at[i, k], r_recv.at[i, k], after)

    for i in range(n):
        reduce_copy(i, 0).start()
    for k in range(ring - 1):
        for i in range(n):
            reduce_copy(i, k).wait_recv()
            mine = ins[i][chunk(k + 2)].astype(jnp.float32)
            total = (mine + lands[i][k].astype(jnp.float32)).astype(lands[i].dtype)
            lands[i][k] = total
            if k < ring - 2:
                reduce_copy(i, k + 1).start()
            elif modes[i] == KEEP:
                outs[i][place] = total

    def swap_copy(i, k, source):
        target = lax.rem(me + k, size)
        return push(
            lands[i].at[ring - 2, target], swaps[i].at[source],
            s_send.at[i, k], s_recv.at[i, source], (replica, target),
        )

    for i in range(n):
        if modes[i] != KEEP:
            for k in range(1, size):
                swap_copy(i, k, me).start()
            swaps[i][me] = lands[i][ring - 2, me]

    def gather_copy(i, k):
        return push(
            outs[i].at[chunk(k)], outs[i].at[chunk(k)], a_send.at[i, k], a_recv.at[i, k], after
        )

    def arrival(i, k):
        return push(
            outs[i].at[chunk(k + 1)], outs[i].at[chunk(k + 1)], a_send.at[i, k], a_recv.at[i, k], after
        )

    order = [i for i in range(n) if modes[i] == KEEP] + [i for i in range(n) if modes[i] != KEEP]
    for i in order:
        if modes[i] != KEEP:
            for k in range(1, size):
                swap_copy(i, size - k, lax.rem(me + k, size)).wait_recv()
            if modes[i] == SWAP:
                outs[i][place] = swaps[i][...]
            else:
                outs[i][place] = jnp.sum(swaps[i][...], axis=0)
        gather_copy(i, 0).start()
    for k in range(ring - 1):
        for i in order:
            arrival(i, k).wait_recv()
            if k < ring - 2:
                gather_copy(i, k + 1).start()
    for i in range(n):
        for k in range(ring - 1):
            reduce_copy(i, k).wait_send()
            gather_copy(i, k).wait_send()
        if modes[i] != KEEP:
            for k in range(1, size):
                swap_copy(i, k, me).wait_send()


def closing(size, ring, arrays, modes):
    dma = pltpu.SemaphoreType.DMA
    n = len(arrays)
    shapes, lands, swaps = [], [], []
    for array, mode in zip(arrays, modes):
        out = array.shape if mode != ADD else array.shape[:1] + array.shape[2:]
        shapes.append(jax.ShapeDtypeStruct(out, array.dtype))
        lands.append(pltpu.VMEM((ring - 1,) + array.shape[1:], array.dtype))
        swaps.append(
            pltpu.VMEM(array.shape[1:] if mode != KEEP else (8, 128), array.dtype)
        )
    return pl.pallas_call(
        functools.partial(closing_kernel, size, ring, modes),
        out_shape=tuple(shapes),
        in_specs=vmem_specs(n),
        out_specs=tuple(vmem_specs(n)),
        scratch_shapes=lands + swaps + [
            dma((n, ring)), dma((n, ring)), dma((n, ring)), dma((n, ring)), dma((n, size)), dma((n, size)),
        ],
        compiler_params=pltpu.CompilerParams(
            collective_id=5, has_side_effects=True, vmem_limit_bytes=VMEM_LIMIT
        ),
    )(*arrays)


def local(
    ring,
    size,
    hidden_in,
    out_grad,
    lengths,
    norm1_gain,
    norm1_bias,
    qkv_weight,
    query_bias,
    value_bias,
    out_weight,
    out_bias,
    norm2_gain,
    norm2_bias,
    up_weight,
    up_bias,
    down_weight,
    down_bias,
):
    me = lax.axis_index("shard")
    rows, width = hidden_in.shape
    band = width // size
    seqs = lengths.shape[1]
    lane_count = max(band, 128)
    wide = lambda vector: jnp.pad(vector, (0, lane_count - vector.shape[0]))
    params = jnp.stack(
        [
            wide(v)
            for v in (
                norm1_gain, norm1_bias, out_bias, norm2_gain, norm2_bias, down_bias,
                lengths[0].astype(jnp.bfloat16), norm1_gain,
            )
        ]
    )
    qkv_parts = qkv_weight.reshape(2, band // 2, 3, size, band).transpose(3, 0, 1, 2, 4)
    qkv_parts = qkv_parts.reshape(size, 2, band // 2, 3 * band)
    ff_band = up_weight.shape[1] // size
    up_parts = up_weight.reshape(2, band // 2, size, ff_band).transpose(2, 0, 1, 3)
    hidden_all, upstream_all, params_all, qkv_all, up_all = opening(
        size, hidden_in, out_grad, params, qkv_parts, up_parts
    )
    hidden_all = hidden_all.reshape(size * rows, width)
    grad_all = upstream_all.reshape(size * rows, width)
    qkv_cols = qkv_all.reshape(width, 3 * band)
    up_cols = up_all.reshape(width, ff_band)
    gain_one, bias_one, outb_full, gain_two, bias_two, downb_full = (
        params_all[:, i, :band].reshape(width) for i in range(6)
    )
    lengths_all = params_all[:, 6, :seqs].astype(jnp.int32)
    mine = lambda array: lax.dynamic_slice_in_dim(array, me * band, band, axis=array.ndim - 1)
    own_rows = lambda array: lax.dynamic_slice_in_dim(array, me * rows, rows, axis=0)

    allowed = seq_mask(lengths_all, rows)
    inputs_wide = hidden_all.astype(jnp.float32)
    first_out, normed_one, inv_one = layer_norm(inputs_wide, gain_one, bias_one)
    first_in = first_out.astype(jnp.bfloat16)
    projected = product(first_in, qkv_cols)
    queries = (projected[:, :band] + query_bias.astype(jnp.float32)).astype(jnp.bfloat16)
    key_rows = projected[:, band : 2 * band].astype(jnp.bfloat16)
    values = (projected[:, 2 * band :] + value_bias.astype(jnp.float32)).astype(jnp.bfloat16)
    context, log_total = attend_forward(queries, key_rows, values, allowed)
    (attended,) = group_sum(
        size, [product(context, out_weight).astype(jnp.bfloat16)], (True,), 1
    )
    residual = (
        inputs_wide
        + attended.reshape(size * rows, width).astype(jnp.float32)
        + outb_full.astype(jnp.float32)
    )
    second_out, normed_two, inv_two = layer_norm(residual, gain_two, bias_two)
    second_in = second_out.astype(jnp.bfloat16)
    pre_act = product(second_in, up_cols) + up_bias.astype(jnp.float32)
    activ_value, gelu_slope = gelu_parts(pre_act)
    activated = activ_value.astype(jnp.bfloat16)
    down_part = product(activated, down_weight).astype(jnp.bfloat16)
    upstream = grad_all.astype(jnp.float32)
    pre_grad = right_product(grad_all, down_weight) * gelu_slope
    pre_round = pre_grad.astype(jnp.bfloat16)
    second_part = right_product(pre_round, up_cols).astype(jnp.bfloat16)
    second_sum, down_sum = group_sum(size, [second_part, down_part], (True, False), 2)
    hidden_out = (own_rows(residual) + down_sum + downb_full.astype(jnp.float32)).astype(
        jnp.bfloat16
    )
    down_grad = column_term(activated, grad_all).astype(jnp.bfloat16)
    up_grad = column_term(second_in, pre_round).astype(jnp.bfloat16)
    second_grad = second_sum.reshape(size * rows, width).astype(jnp.float32)
    norm_two_in, gain2_grad, bias2_grad = norm_back(second_grad, normed_two, inv_two, gain_two)
    resid_grad = upstream + norm_two_in
    resid_round = resid_grad.astype(jnp.bfloat16)
    outw_grad = column_term(context, resid_round).astype(jnp.bfloat16)
    context_grad = right_product(resid_round, out_weight).astype(jnp.bfloat16)
    query_grad, key_grad, value_grad = attend_backward(
        queries, key_rows, values, allowed, log_total, context_grad
    )
    qkv_grad = jnp.concatenate([query_grad, key_grad, value_grad], axis=1).astype(jnp.bfloat16)
    first_part = right_product(qkv_grad, qkv_cols).astype(jnp.bfloat16)
    (first_grad,) = group_sum(size, [first_part], (False,), 3)
    qkvw_grad = column_term(first_in, qkv_grad).astype(jnp.bfloat16)
    norm_one_in, gain1_grad, bias1_grad = norm_back(
        first_grad, own_rows(normed_one), own_rows(inv_one), gain_one
    )
    in_grad = (own_rows(resid_grad) + norm_one_in).astype(jnp.bfloat16)

    owned = jnp.concatenate(
        [
            jnp.sum(query_grad, axis=0),
            jnp.sum(value_grad, axis=0),
            mine(jnp.sum(resid_grad, axis=0)),
            mine(gain2_grad),
            mine(bias2_grad),
            jnp.sum(pre_grad, axis=0),
            mine(jnp.sum(upstream, axis=0)),
        ]
    )
    here = (jnp.arange(size) == me)[:, None]
    small = jnp.concatenate(
        [
            gain1_grad.reshape(size, band),
            bias1_grad.reshape(size, band),
            jnp.where(here, owned[None], 0.0),
        ],
        axis=1,
    )
    count = small.shape[1]
    small = small.reshape(size, ring, 1, count // ring).transpose(1, 0, 2, 3)
    slab = band // ring
    by_owner = lambda array: array.reshape(size, ring, slab, array.shape[1]).transpose(1, 0, 2, 3)
    down_all, outw_all, up_total, qkv_total, small_all = closing(
        size,
        ring,
        [
            down_grad.reshape(ring, -1, width),
            outw_grad.reshape(ring, -1, width),
            by_owner(up_grad),
            by_owner(qkvw_grad),
            small,
        ],
        (KEEP, KEEP, SWAP, SWAP, ADD),
    )
    downw_total = down_all.reshape(down_weight.shape).astype(jnp.float32)
    outw_total = outw_all.reshape(out_weight.shape).astype(jnp.float32)
    upw_total = up_total.transpose(0, 2, 1, 3).reshape(up_weight.shape).astype(jnp.float32)
    qkvw_total = (
        qkv_total.reshape(ring, size, slab, 3, band)
        .transpose(0, 2, 3, 1, 4)
        .reshape(qkv_weight.shape)
        .astype(jnp.float32)
    )
    flat = small_all.reshape(count)
    pieces = []
    offset = 0
    for length in (band, band, band, band, band, band, band, ff_band, band):
        pieces.append(flat[offset : offset + length])
        offset += length
    gain1_t, bias1_t, qbias_t, vbias_t, outb_t, gain2_t, bias2_t, upb_t, downb_t = pieces
    return (
        hidden_out,
        in_grad,
        gain1_t,
        bias1_t,
        qkvw_total,
        qbias_t,
        vbias_t,
        outw_total,
        outb_t,
        gain2_t,
        bias2_t,
        upw_total,
        upb_t,
        downw_total,
        downb_t,
    )


def lanes(start, width):
    return pl.ds(pl.multiple_of(start, 128), width)


def entry_kernel(size, splits, hid_ref, grad_ref, par_ref, qkv_ref, up_ref,
                 hid_out, grad_out, par_out, qkv_out, up_out,
                 g_send, g_recv, w_send, w_recv, f_send, local_sem, own_sem):
    replica = lax.axis_index("replica")
    me = lax.axis_index("shard")
    low = lax.rem(replica, 2)
    high = lax.rem(replica // 2, 2)
    part = low + 2 * high
    core = lax.rem(me, 2)
    outer = me // 2
    half = size // 2
    partner = me + 1 - 2 * core
    flips = ((1, 0), (0, 1), (1, 1))
    twins = [replica + a * (1 - 2 * low) + 2 * b * (1 - 2 * high) for a, b in flips]
    theirs = [
        (low + a * (1 - 2 * low)) + 2 * (high + b * (1 - 2 * high)) for a, b in flips
    ]
    weights = ((qkv_ref, qkv_out), (up_ref, up_out))
    own = []
    for i, (src, dst) in enumerate(((hid_ref, hid_out), (grad_ref, grad_out), (par_ref, par_out))):
        own.append(pltpu.make_async_copy(src.at[0], dst.at[me], local_sem.at[i]))
        own[-1].start()

    def views(w, owner, target, which):
        src, dst = weights[w]
        span = src.shape[2] // splits[w]
        wide = span // size
        for j in range(splits[w]):
            yield (
                j,
                src.at[which, :, lanes(j * span + target * wide, wide)],
                dst.at[owner, which, :, pl.ds(j * wide, wide)],
            )

    full = slice(None)
    for w in range(2):
        for j, source, target in views(w, me, me, full):
            own.append(pltpu.make_async_copy(source, target, own_sem.at[w, j]))
            own[-1].start()
    greet(group_peers(replica, me, size) + [(twin, me) for twin in twins])
    spreads = [
        Spread(out, replica, me, size, g_send.at[i], g_recv.at[i])
        for i, out in enumerate((hid_out, grad_out, par_out))
    ]
    own[0].wait()
    own[2].wait()
    spreads[2].start()
    spreads[0].start()
    remote = []
    for k in range(1, half):
        j = lax.rem(outer + k, half)
        remote += [2 * j + core, 2 * j + 1 - core]
    first = []
    for w in range(2):
        for t, target in enumerate(remote):
            for j, source, landing in views(w, me, target, part):
                copy = push(
                    source, landing, w_send.at[w, t, j], w_recv.at[w, me, part, j], (replica, target)
                )
                copy.start()
                first.append(copy)
        for j, source, landing in views(w, me, partner, full):
            copy = push(
                source, landing, w_send.at[w, len(remote), j], w_recv.at[w, me, 0, j],
                (replica, partner),
            )
            copy.start()
            first.append(copy)
    own[1].wait()
    spreads[1].start()
    spreads[2].forward()
    spreads[0].forward()
    second = []
    for w in range(2):
        dst = weights[w][1]
        for t, source in enumerate(remote):
            for j, view, landing in views(w, source, me, part):
                push(
                    view, landing, w_send.at[w, t, j], w_recv.at[w, source, part, j], (replica, source)
                ).wait_recv()
            for m, twin in enumerate(twins):
                copy = push(
                    dst.at[source, part], dst.at[source, part],
                    f_send.at[w, t, m], w_recv.at[w, source, part, 0], (twin, me),
                )
                copy.start()
                second.append(copy)
    spreads[1].forward()
    for w in range(2):
        dst = weights[w][1]
        for source in remote:
            for m, twin in enumerate(twins):
                push(
                    dst.at[source, theirs[m]], dst.at[source, theirs[m]],
                    f_send.at[w, 0, m], w_recv.at[w, source, theirs[m], 0], (twin, me),
                ).wait_recv()
        for j, view, landing in views(w, partner, me, full):
            push(
                view, landing, w_send.at[w, 0, j], w_recv.at[w, partner, 0, j], (replica, partner)
            ).wait_recv()
    for copy in first + second:
        copy.wait_send()
    for copy in own[3:]:
        copy.wait()
    for spread in spreads:
        spread.finish()


def entry(size, hidden, upstream, params, qkv_weight, up_weight):
    dma = pltpu.SemaphoreType.DMA
    band = qkv_weight.shape[0]
    shape = lambda array: jax.ShapeDtypeStruct((size,) + array.shape[1:], array.dtype)
    gathers = (hidden[None], upstream[None], params[None])
    weights = tuple(w.reshape(4, band // 4, w.shape[1]) for w in (qkv_weight, up_weight))
    outs = tuple(shape(a) for a in gathers) + tuple(
        jax.ShapeDtypeStruct((size, 4, band // 4, w.shape[2] // size), w.dtype) for w in weights
    )
    return pl.pallas_call(
        functools.partial(entry_kernel, size, (3, 1)),
        out_shape=outs,
        in_specs=[pl.BlockSpec(memory_space=pl.ANY)] * 5,
        out_specs=tuple(vmem_specs(5)),
        scratch_shapes=[
            dma((3, size)), dma((3, size)), dma((2, size, 3)), dma((2, size, 4, 3)),
            dma((2, size, 3)), dma((3,)), dma((2, 3)),
        ],
        compiler_params=pltpu.CompilerParams(
            collective_id=0, has_side_effects=True, vmem_limit_bytes=VMEM_LIMIT
        ),
    )(*gathers, *weights)


class Where:
    def __init__(self, size, ring):
        self.size, self.ring = size, ring
        self.replica = lax.axis_index("replica")
        self.me = lax.axis_index("shard")
        self.core = lax.rem(self.me, 2)
        self.outer = self.me // 2
        self.half = size // 2
        self.partner = (self.replica, self.me + 1 - 2 * self.core)
        self.order = [lax.rem(self.outer + k, self.half) for k in range(1, self.half)] + [self.outer]
        side = lax.rem(self.replica, 2)
        depth = self.replica // 2
        self.place = (1 - side) * depth + side * (ring - 1 - depth)
        self.step = 1 - 2 * self.core
        self.after = (self.member(self.place + self.step), self.me)
        self.before = (self.member(self.place - self.step), self.me)

    def member(self, position):
        ring = self.ring
        position = lax.rem(position + 2 * ring, ring)
        late = position // (ring // 2)
        return (1 - late) * 2 * position + late * (2 * (ring - 1 - position) + 1)

    def chunk(self, hops):
        return lax.rem(self.place - self.step * hops + 2 * self.ring, self.ring)


class Ring:
    def __init__(self, where, i, source, land, out, swap, sems, mode, pieces=1):
        self.where, self.source, self.land, self.out, self.swap = where, source, land, out, swap
        self.r_send, self.r_recv, self.a_send, self.a_recv, self.s_send, self.s_recv = (
            sem.at[i] for sem in sems
        )
        self.mode, self.pieces = mode, pieces
        self.last = where.ring - 2

    def block(self, position):
        return self.source.at[:, position] if self.mode == SWAP else self.source.at[position]

    def reduce_copy(self, k):
        source = self.block(self.where.chunk(1)) if k == 0 else self.land.at[k - 1]
        return push(source, self.land.at[k], self.r_send.at[k], self.r_recv.at[k], self.where.after)

    def swap_copy(self, k, source):
        where = self.where
        target = lax.rem(where.me + k, where.size)
        return push(
            self.land.at[self.last, target], self.swap.at[source],
            self.s_send.at[k], self.s_recv.at[source], (where.replica, target),
        )

    def gather_copy(self, k, hops):
        part = self.spot(self.where.chunk(hops))
        return push(part, part, self.a_send.at[k], self.a_recv.at[k], self.where.after)

    def spot(self, position):
        if self.mode != ADD:
            return self.out.at[position]
        wide = self.land.shape[-1]
        return self.out.at[:, lanes(position * wide, wide)]

    def start(self):
        self.reduce_copy(0).start()

    def reduce_step(self, k):
        where, land = self.where, self.land
        self.reduce_copy(k).wait_recv()
        position = where.chunk(k + 2)
        mine = self.source[:, position] if self.mode == SWAP else self.source[position]
        total = (mine.astype(ADDS) + land[k].astype(ADDS)).astype(land.dtype)
        land[k] = total
        if k < self.last:
            self.reduce_copy(k + 1).start()
        elif self.mode == KEEP:
            self.out[where.place] = total
            self.gather_copy(0, 0).start()
        else:
            for step in range(1, where.size):
                self.swap_copy(step, where.me).start()
            self.swap[where.me] = land[k, where.me]

    def turn(self):
        where = self.where
        if self.mode == KEEP:
            return
        for k in range(1, where.size):
            self.swap_copy(where.size - k, lax.rem(where.me + k, where.size)).wait_recv()
        if self.mode == ADD:
            self.spot(where.place)[...] = jnp.sum(self.swap[...], axis=0)
        else:
            wide = self.land.shape[-1] // self.pieces
            for s in range(where.size):
                for j in range(self.pieces):
                    start = (j * where.size + s) * wide
                    self.out[where.place, :, start : start + wide] = self.swap[
                        s, :, j * wide : (j + 1) * wide
                    ]
        self.gather_copy(0, 0).start()

    def gather_step(self, k):
        self.gather_copy(k, k + 1).wait_recv()
        if k < self.last:
            self.gather_copy(k + 1, k + 1).start()

    def stages(self):
        steps = [functools.partial(self.reduce_step, k) for k in range(self.last + 1)]
        if self.mode != KEEP:
            steps.append(self.turn)
        return steps + [functools.partial(self.gather_step, k) for k in range(self.last + 1)]

    def drain(self):
        for k in range(self.last + 1):
            self.reduce_copy(k).wait_send()
            self.gather_copy(k, k).wait_send()
        if self.mode != KEEP:
            for k in range(1, self.where.size):
                self.swap_copy(k, self.where.me).wait_send()


class GroupSum:
    def __init__(self, where, source, near, summed, far, sems):
        self.where, self.source, self.near, self.summed, self.far = where, source, near, summed, far
        self.p_send, self.p_recv, self.x_send, self.x_recv = sems

    def near_copy(self, k):
        j = self.where.order[k]
        return push(
            self.source.at[2 * j + 1 - self.where.core], self.near.at[j],
            self.p_send.at[k], self.p_recv.at[j], self.where.partner,
        )

    def far_copy(self, k, landing):
        where = self.where
        return push(
            self.summed.at[k], self.far.at[landing], self.x_send.at[k], self.x_recv.at[landing],
            (where.replica, 2 * where.order[k] + where.core),
        )

    def send(self, k):
        self.near_copy(k).start()

    def reduce(self, k):
        where = self.where
        j = where.order[k]
        self.near_copy(k).wait_recv()
        block = self.source[2 * j + where.core].astype(jnp.float32) + self.near[j].astype(jnp.float32)
        self.summed[k] = block.astype(jnp.bfloat16)
        self.far_copy(k, where.outer).start()

    def arrive(self):
        self.near_copy(self.where.half - 1).wait_recv()
        for k in range(self.where.half - 1):
            self.far_copy(k, self.where.order[k]).wait_recv()

    def tile(self, rows):
        where = self.where
        total = self.source[where.me, rows].astype(jnp.float32) + self.near[
            where.outer, rows
        ].astype(jnp.float32)
        for j in where.order[:-1]:
            total = total + self.far[j, rows].astype(jnp.float32)
        return total

    def drain(self):
        for k in range(self.where.half):
            self.near_copy(k).wait_send()
            if k < self.where.half - 1:
                self.far_copy(k, self.where.outer).wait_send()


TILE = 16
PAIR_SERVE = 0
SPLIT = 2
ADDS = jnp.float32
LATE_RATE = 1


def tiles(count, body):
    @pl.loop(0, count // TILE)
    def _(t):
        body(pl.ds(pl.multiple_of(t * TILE, TILE), TILE))


def fold(value):
    return jnp.sum(value.reshape(TILE // 8, 8, value.shape[-1]), axis=0)


def row_stats(inputs):
    average = jnp.mean(inputs, axis=-1, keepdims=True)
    centred = inputs - average
    inv_std = lax.rsqrt(jnp.mean(centred * centred, axis=-1, keepdims=True) + EPSILON)
    return (centred * inv_std, inv_std)


def row_back(upstream, normed, inv_std, gain_row):
    scaled = upstream * gain_row
    first_term = jnp.mean(scaled, axis=-1, keepdims=True)
    second_term = jnp.mean(scaled * normed, axis=-1, keepdims=True)
    return inv_std * (scaled - first_term - normed * second_term)


def back_kernel(size, ring,
                act_ref, pre_ref, grad_ref, vec_ref, upb_ref,
                sec_hbm, upw_hbm, dnw_hbm, resid_hbm, hid_hbm,
                q_hbm, k_hbm, v_hbm, allow_hbm, ctx_hbm, outw_hbm, first_hbm, qkvw_hbm,
                hidden_out, in_out, down_out, outw_out, up_out, qkv_out, small_out,
                sec_ref, upw_ref, dnw_ref, resid_ref, hid_ref,
                q_ref, k_ref, v_ref, allow_ref, ctx_ref, outw_ref, first_ref, qkvw_ref,
                second_ref, down_ref, dgrad_ref, ugrad_ref, load_sem,
                near_a, summed_a, far_a, near_b, summed_b, far_b, near_c, summed_c, far_c,
                ssum, fpart, rgrad, rround, qkvg, outg, qkvwg, small, acc, bias,
                land_d, land_o, land_u, land_q, land_s, swap_u, swap_q, swap_s,
                p_send, p_recv, x_send, x_recv, g_send, g_recv,
                r_send, r_recv, a_send, a_recv, s_send, s_recv):
    where = Where(size, ring)
    me, replica = where.me, where.replica
    rows, width = hid_ref.shape
    band = q_ref.shape[2]
    slab = band // ring
    scale_factor = 1.0 / math.sqrt(HEAD_DIM)
    loads = [
        pltpu.make_async_copy(source, target, load_sem.at[i])
        for i, (source, target) in enumerate(
            (
                (sec_hbm, sec_ref), (upw_hbm, upw_ref), (resid_hbm, resid_ref), (dnw_hbm, dnw_ref),
                (ctx_hbm, ctx_ref), (outw_hbm, outw_ref), (q_hbm, q_ref), (k_hbm, k_ref),
                (v_hbm, v_ref), (allow_hbm, allow_ref), (qkvw_hbm, qkvw_ref), (first_hbm, first_ref),
                (hid_hbm, hid_ref),
            )
        )
    ]
    for load in loads:
        load.start()
    greet(group_peers(replica, me, size) + [where.after, where.before])
    flat = lambda value: value.reshape(size * rows, value.shape[-1])
    sems = (r_send, r_recv, a_send, a_recv, s_send, s_recv)
    index = iter(range(r_send.shape[0]))

    def rings(source, land, out, swap, mode, count, pieces=1):
        made = []
        deep = out.shape[1] // count
        for n in range(count):
            part = pl.ds(n * deep, deep)
            views = (
                (source.at[:, part], land.at[:, part], out.at[:, part], None)
                if mode == KEEP
                else (source.at[:, :, part], land.at[:, :, part], out.at[:, part], swap.at[:, part])
            )
            made.append(Ring(where, next(index), *views, sems, mode, pieces))
        return made

    down_rings = rings(dgrad_ref, land_d, down_out, None, KEEP, SPLIT)
    up_rings = rings(ugrad_ref, land_u, up_out, swap_u, SWAP, SPLIT)
    outw_rings = rings(outg, land_o, outw_out, None, KEEP, 1)
    qkv_rings = rings(qkvwg, land_q, qkv_out, swap_q, SWAP, SPLIT, 3)
    small_ring = Ring(where, next(index), small, land_s, small_out, swap_s, sems, ADD)
    all_rings = down_rings + up_rings + outw_rings + qkv_rings + [small_ring]

    def launch(made):
        for ring_ in made:
            ring_.start()

    def woven(queues):
        queues = [list(queue) for queue in queues]
        order = []
        while any(queues):
            for queue in queues:
                if queue:
                    order.append(queue.pop(0))
        return order

    stages_of = lambda made: [ring_.stages() for ring_ in made]
    sums = []
    for i, buffers in enumerate(
        (
            (second_ref, near_a, summed_a, far_a),
            (down_ref, near_b, summed_b, far_b),
            (fpart, near_c, summed_c, far_c),
        )
    ):
        sums.append(
            GroupSum(where, *buffers, (p_send.at[i], p_recv.at[i], x_send.at[i], x_recv.at[i]))
        )
    second_sum, down_sum, first_sum = sums
    half = where.half

    deep = dgrad_ref.shape[1]

    def down_chunk(hops):
        position = where.chunk(hops)
        grad = left_product(act_ref[:, lanes(position * deep, deep)], flat(grad_ref[...]))
        dgrad_ref[position] = grad.astype(jnp.bfloat16)

    def own_rows(block):
        return pl.ds(pl.multiple_of(block * rows, rows), rows)

    def second_block(block):
        grad = right_product(pre_ref[own_rows(block)], upw_ref[...])
        second_ref[block] = grad.astype(jnp.bfloat16)

    def down_block(block):
        part = product(act_ref[own_rows(block)], dnw_ref[...])
        down_ref[block] = part.astype(jnp.bfloat16)

    down_chunk(1)
    launch(down_rings)
    loads[0].wait()

    @pl.loop(0, size)
    def _(t):
        grad = left_product(sec_ref[:, lanes(t * band, band)], pre_ref[...])
        ugrad_ref[t] = grad.astype(jnp.bfloat16).reshape(ugrad_ref.shape[1:])

    launch(up_rings)
    loads[1].wait()
    for k in range(half):
        second_block(2 * where.order[k] + 1 - where.core)
        second_sum.send(k)

    @pl.loop(2, ring + 1)
    def _(hops):
        down_chunk(hops)

    for k in range(half):
        second_block(2 * where.order[k] + where.core)
    ffn_rings = [ring_ for pair in zip(down_rings, up_rings) for ring_ in pair]
    early = woven(stages_of(ffn_rings))

    def serve(count):
        for _ in range(count * SPLIT):
            if early:
                early.pop(0)()

    for k in range(half - 1):
        second_sum.reduce(k)
    acc[...] = jnp.zeros_like(acc)
    bias[...] = jnp.zeros_like(bias)
    small[...] = jnp.zeros_like(small)
    serve(2)
    second_sum.arrive()

    def second_total(part):
        ssum[me, part] = second_sum.tile(part).astype(jnp.bfloat16)

    tiles(rows, second_total)
    spread = Spread(ssum, replica, me, size, g_send, g_recv)
    spread.start()
    loads[2].wait()
    serve(1)

    def norm_two(block):
        def body(part):
            normed, inv_std = row_stats(resid_ref[block, part])
            upper = ssum[block, part].astype(jnp.float32)
            total = grad_ref[block, part].astype(jnp.float32) + row_back(
                upper, normed, inv_std, vec_ref[1:2]
            )
            rgrad[block, part] = total
            rround[block, part] = total.astype(jnp.bfloat16)
            acc[0] += fold(upper * normed)
            acc[1] += fold(upper)
            acc[2] += fold(total)

        tiles(rows, body)

    norm_two(me)
    serve(1)
    spread.forward()
    serve(1)
    spread.finish()
    for k in range(1, size):
        norm_two(lax.rem(me + k, size))
        serve(1)

    loads[4].wait()

    @pl.loop(0, width // 256)
    def _(t):
        cut = lanes(t * 256, 256)
        grad = left_product(flat(ctx_ref[...]), flat(rround[:, :, cut]))
        outg[:, :, cut] = grad.astype(jnp.bfloat16).reshape(ring, slab, 256)

    launch(outw_rings)
    loads[3].wait()
    for k in range(half):
        down_block(2 * where.order[k] + 1 - where.core)
        down_sum.send(k)
    for k in range(half):
        down_block(2 * where.order[k] + where.core)
    for k in range(half - 1):
        down_sum.reduce(k)
    outw_stages = woven(stages_of(outw_rings))
    merged = []
    for i, stage in enumerate(early):
        merged.append(stage)
        if i % (2 * SPLIT) == 2 * SPLIT - 1 and outw_stages:
            merged.append(outw_stages.pop(0))
    early[:] = merged + outw_stages
    serve(1)


    lane = lax.broadcasted_iota(jnp.int32, (rows, 128), 1)
    sides = [(lane < HEAD_DIM), (lane >= HEAD_DIM)]
    masks = [side.astype(jnp.float32).astype(jnp.bfloat16) for side in sides]

    def block_back(block):
        context_grad = right_product(rround[block], outw_ref[...]).astype(jnp.bfloat16)
        visible = allow_ref[block] > 0.5
        cuts = [slice(pair * 128, (pair + 1) * 128) for pair in range(band // 128)]
        heads = [(cut, mask) for cut in cuts for mask in masks]
        keys = {cut.start: k_ref[block, :, cut] for cut in cuts}
        scores = [
            right_product(q_ref[block, :, cut] * mask, keys[cut.start]) * scale_factor
            for cut, mask in heads
        ]
        prob_grads = [
            right_product(context_grad[:, cut] * mask, v_ref[block, :, cut]) for cut, mask in heads
        ]
        totals = [
            jnp.sum(jnp.where(visible, jnp.exp(score), 0.0), axis=-1, keepdims=True) for score in scores
        ]
        probs = [
            jnp.where(visible, jnp.exp(score - jnp.log(total)), 0.0)
            for score, total in zip(scores, totals)
        ]
        rounded = [prob.astype(jnp.bfloat16) for prob in probs]
        deltas = [
            jnp.sum(prob * grad, axis=-1, keepdims=True) for prob, grad in zip(probs, prob_grads)
        ]
        score_grads = [
            (prob * (grad - delta) * scale_factor).astype(jnp.bfloat16)
            for prob, grad, delta in zip(probs, prob_grads, deltas)
        ]
        groups = [
            [product(sg, keys[cut.start]) for sg, (cut, _) in zip(score_grads, heads)],
            [left_product(sg, q_ref[block, :, cut]) for sg, (cut, _) in zip(score_grads, heads)],
            [left_product(pr, context_grad[:, cut]) for pr, (cut, _) in zip(rounded, heads)],
        ]
        for j, group in enumerate(groups):
            for pair in range(band // 128):
                grad = jnp.where(sides[0], group[2 * pair], group[2 * pair + 1])
                start = j * band + pair * 128
                qkvg[block, :, start : start + 128] = grad.astype(jnp.bfloat16)
                if j != 1:
                    bias[:, start : start + 128] += jnp.sum(
                        grad.reshape(rows // 8, 8, 128), axis=0
                    )
        serve(PAIR_SERVE)
        fpart[block] = right_product(qkvg[block], qkvw_ref[...]).astype(jnp.bfloat16)

    for load in loads[5:]:
        load.wait()
    for k in range(half):
        block_back(2 * where.order[k] + 1 - where.core)
        first_sum.send(k)
        serve(1)
    for k in range(half):
        block_back(2 * where.order[k] + where.core)
        if k < half - 1:
            first_sum.reduce(k)
        serve(1)

    @pl.loop(0, size)
    def _(t):
        grad = left_product(flat(first_ref[:, :, lanes(t * band, band)]), flat(qkvg[...]))
        qkvwg[t] = grad.astype(jnp.bfloat16).reshape(ring, slab, 3 * band)

    launch(qkv_rings)
    serve(2)
    first_sum.arrive()

    def norm_one(part):
        normed, inv_std = row_stats(hid_ref[part].astype(jnp.float32))
        upper = first_sum.tile(part)
        total = rgrad[me, part] + row_back(upper, normed, inv_std, vec_ref[0:1])
        in_out[part] = total.astype(jnp.bfloat16)
        acc[3] += fold(upper * normed)
        acc[4] += fold(upper)

    tiles(rows, norm_one)
    serve(1)
    down_sum.arrive()

    def finish_hidden(part):
        total = resid_ref[me, part] + down_sum.tile(part) + vec_ref[2:3]
        hidden_out[part] = total.astype(jnp.bfloat16)

    tiles(rows, finish_hidden)
    serve(1)

    span = small.shape[3]

    def put(owner, start, row):
        for t in range(row.shape[1] // 128):
            position = start + t * 128
            small[position // span, owner, :, position % span : position % span + 128] = row[
                :, t * 128 : (t + 1) * 128
            ]

    for i in range(2):
        line = jnp.sum(acc[3 + i], axis=0, keepdims=True)
        for s in range(size):
            put(s, i * band, line[:, s * band : (s + 1) * band])
    start = 2 * band
    line = jnp.sum(bias[...], axis=0, keepdims=True)
    put(me, start, line[:, :band])
    put(me, start + band, line[:, 2 * band :])
    start += 2 * band
    for i in (2, 0, 1):
        put(me, start, jnp.sum(acc[i, :, lanes(me * band, band)], axis=0, keepdims=True))
        start += band
    put(me, start, upb_ref[...])
    start += upb_ref.shape[1]
    put(me, start, vec_ref[3:4, lanes(me * band, band)])
    small_ring.start()

    late = woven(stages_of(qkv_rings + [small_ring]))
    share = max(1, round(len(early) / max(1, len(late)) * LATE_RATE))
    while early or late:
        for _ in range(share):
            if early:
                early.pop(0)()
        for _ in range(LATE_RATE):
            if late:
                late.pop(0)()
    for part in sums + all_rings:
        part.drain()


def back(size, ring, arrays, small_count):
    dma = pltpu.SemaphoreType.DMA
    (act, pre, grads, vec, upb) = arrays[:5]
    moved = arrays[5:]
    rows, width = moved[4].shape
    band = moved[5].shape[2]
    slab = band // ring
    half = size // 2
    ff_band = act.shape[1]
    b16, f32 = jnp.bfloat16, jnp.float32
    vm = pltpu.VMEM
    scratch = [vm(array.shape, array.dtype) for array in moved]
    scratch += [
        vm((size, rows, width), b16),
        vm((size, rows, width), b16),
        vm((ring, ff_band // ring, width), b16),
        vm((size, ring, slab, ff_band), b16),
        dma((len(moved),)),
    ]
    scratch += [vm((half, rows, width), b16)] * 9
    scratch += [
        vm((size, rows, width), b16),
        vm((size, rows, width), b16),
        vm((size, rows, width), f32),
        vm((size, rows, width), b16),
        vm((size, rows, 3 * band), b16),
        vm((ring, slab, width), b16),
        vm((size, ring, slab, 3 * band), b16),
        vm((ring, size, 1, small_count // ring), f32),
        vm((5, 8, width), f32),
        vm((8, 3 * band), f32),
        vm((ring - 1, ff_band // ring, width), b16),
        vm((ring - 1, slab, width), b16),
        vm((ring - 1, size, slab, ff_band), b16),
        vm((ring - 1, size, slab, 3 * band), b16),
        vm((ring - 1, size, 1, small_count // ring), f32),
        vm((size, slab, ff_band), b16),
        vm((size, slab, 3 * band), b16),
        vm((size, 1, small_count // ring), f32),
    ]
    scratch += [dma((3, half))] * 4 + [dma((size,))] * 2 + [dma((8, ring))] * 4 + [dma((8, size))] * 2
    shape = jax.ShapeDtypeStruct
    outs = (
        shape((rows, width), b16),
        shape((rows, width), b16),
        shape((ring, ff_band // ring, width), b16),
        shape((ring, slab, width), b16),
        shape((ring, slab, size * ff_band), b16),
        shape((ring, slab, 3 * width), b16),
        shape((1, small_count), f32),
    )
    return pl.pallas_call(
        functools.partial(back_kernel, size, ring),
        out_shape=outs,
        in_specs=vmem_specs(5) + [pl.BlockSpec(memory_space=pl.ANY)] * len(moved),
        out_specs=tuple(vmem_specs(len(outs))),
        scratch_shapes=scratch,
        compiler_params=pltpu.CompilerParams(
            collective_id=2, has_side_effects=True, vmem_limit_bytes=VMEM_LIMIT
        ),
    )(*arrays)


def fused(
    ring,
    size,
    hidden_in,
    out_grad,
    lengths,
    norm1_gain,
    norm1_bias,
    qkv_weight,
    query_bias,
    value_bias,
    out_weight,
    out_bias,
    norm2_gain,
    norm2_bias,
    up_weight,
    up_bias,
    down_weight,
    down_bias,
):
    rows, width = hidden_in.shape
    band = width // size
    seqs = lengths.shape[1]
    ff_band = up_weight.shape[1] // size
    params = layer_rows(
        (
            norm1_gain, norm1_bias, out_bias, norm2_gain, norm2_bias, down_bias,
            jnp.pad(lengths[0].astype(jnp.bfloat16), (0, band - seqs)),
        ),
        8,
    )
    hidden_all, upstream_all, params_all, qkv_all, up_all = entry(
        size, hidden_in, out_grad, params, qkv_weight, up_weight
    )
    hidden_all = hidden_all.reshape(size * rows, width)
    grad_all = upstream_all.reshape(size * rows, width)
    qkv_cols = qkv_all.reshape(width, 3 * band)
    up_cols = up_all.reshape(width, ff_band)
    gain_one, bias_one, outb_full, gain_two, bias_two, downb_full = (
        params_all[:, i, :band].reshape(width) for i in range(6)
    )
    lengths_all = params_all[:, 6, :seqs].astype(jnp.int32)

    allowed = seq_mask(lengths_all, rows)
    inputs_wide = hidden_all.astype(jnp.float32)
    first_out, _, _ = layer_norm(inputs_wide, gain_one, bias_one)
    first_in = first_out.astype(jnp.bfloat16)
    projected = product(first_in, qkv_cols)
    queries = (projected[:, :band] + query_bias.astype(jnp.float32)).astype(jnp.bfloat16)
    key_rows = projected[:, band : 2 * band].astype(jnp.bfloat16)
    values = (projected[:, 2 * band :] + value_bias.astype(jnp.float32)).astype(jnp.bfloat16)
    by_block = lambda array: array.reshape(size, rows, array.shape[-1])
    allow = allowed.astype(jnp.float32)
    context = attend(by_block(queries), by_block(key_rows), by_block(values), allow)
    (attended,) = group_sum(
        size,
        [product(context.reshape(size * rows, band), out_weight).astype(jnp.bfloat16)],
        (True,),
        1,
    )
    residual = (
        inputs_wide
        + attended.reshape(size * rows, width).astype(jnp.float32)
        + outb_full.astype(jnp.float32)
    )
    second_out, _, _ = layer_norm(residual, gain_two, bias_two)
    second_in = second_out.astype(jnp.bfloat16)
    pre_act = product(second_in, up_cols) + up_bias.astype(jnp.float32)
    activ_value, gelu_slope = gelu_parts(pre_act)
    activated = activ_value.astype(jnp.bfloat16)
    upstream = grad_all.astype(jnp.float32)
    pre_grad = right_product(grad_all, down_weight) * gelu_slope
    pre_round = pre_grad.astype(jnp.bfloat16)
    vectors = layer_rows(
        (
            gain_one.astype(jnp.float32),
            gain_two.astype(jnp.float32),
            downb_full.astype(jnp.float32),
            jnp.sum(upstream, axis=0),
        ),
        8,
    )
    slab = band // ring
    lengths_out = (band, band, band, band, band, band, band, ff_band, band)
    hidden_out, in_grad, down_all, outw_all, up_total, qkv_total, small_all = back(
        size,
        ring,
        (
            activated,
            pre_round,
            by_block(grad_all),
            vectors,
            jnp.sum(pre_grad, axis=0)[None],
            second_in,
            up_cols,
            down_weight,
            by_block(residual),
            hidden_in,
            by_block(queries),
            by_block(key_rows),
            by_block(values),
            allow,
            context,
            out_weight,
            by_block(first_in),
            qkv_cols,
        ),
        sum(lengths_out),
    )
    final = lambda array, like: array.reshape(like.shape).astype(jnp.float32)
    flat = small_all.reshape(-1)
    pieces = []
    offset = 0
    for length in lengths_out:
        pieces.append(flat[offset : offset + length])
        offset += length
    gain1_t, bias1_t, qbias_t, vbias_t, outb_t, gain2_t, bias2_t, upb_t, downb_t = pieces
    return (
        hidden_out,
        in_grad,
        gain1_t,
        bias1_t,
        final(qkv_total, qkv_weight),
        qbias_t,
        vbias_t,
        final(outw_all, out_weight),
        outb_t,
        gain2_t,
        bias2_t,
        final(up_total, up_weight),
        upb_t,
        final(down_all, down_weight),
        downb_t,
    )


def layer_rows(vectors, count):
    place = lax.broadcasted_iota(jnp.int32, (count, vectors[0].shape[0]), 0)
    rows = jnp.zeros(place.shape, vectors[0].dtype)
    for i, vector in enumerate(vectors):
        rows = jnp.where(place == i, vector[None], rows)
    return rows


def attend_kernel(q_ref, k_ref, v_ref, allow_ref, ctx_ref):
    rows, band = q_ref.shape[1:]
    lane = lax.broadcasted_iota(jnp.int32, (rows, 128), 1)
    sides = [(lane < HEAD_DIM), (lane >= HEAD_DIM)]
    masks = [side.astype(jnp.float32).astype(jnp.bfloat16) for side in sides]

    @pl.loop(0, q_ref.shape[0])
    def _(block):
        visible = allow_ref[block] > 0.5
        cuts = [slice(pair * 128, (pair + 1) * 128) for pair in range(band // 128)]
        scores = [
            right_product(q_ref[block, :, cut] * mask, k_ref[block, :, cut])
            * (1.0 / math.sqrt(HEAD_DIM))
            for cut in cuts
            for mask in masks
        ]
        totals = [
            jnp.sum(jnp.where(visible, jnp.exp(score), 0.0), axis=-1, keepdims=True) for score in scores
        ]
        probs = [
            jnp.where(visible, jnp.exp(score - jnp.log(total)), 0.0).astype(jnp.bfloat16)
            for score, total in zip(scores, totals)
        ]
        for i, cut in enumerate(cuts):
            value = v_ref[block, :, cut]
            ctx_ref[block, :, cut] = jnp.where(
                sides[0], product(probs[2 * i], value), product(probs[2 * i + 1], value)
            ).astype(jnp.bfloat16)


def attend(queries, key_rows, values, allow):
    return pl.pallas_call(
        attend_kernel,
        out_shape=jax.ShapeDtypeStruct(queries.shape, queries.dtype),
        in_specs=vmem_specs(4),
        out_specs=vmem_specs(1)[0],
    )(queries, key_rows, values, allow)


def choose(ring, size, hidden_in, *rest):
    rows, width = hidden_in.shape
    band = width // size
    aligned = width % size == 0 and band % 256 == 0 and band % (16 * ring) == 0
    body = fused if aligned and rows % 128 == 0 and size % 2 == 0 and ring % 4 == 0 else local
    return body(ring, size, hidden_in, *rest)


def solution(mesh):
    in_specs = (
        P(("replica", "shard"), None),
        P(("replica", "shard"), None),
        P(("replica", "shard"), None),
        P("shard"),
        P("shard"),
        P("shard", None),
        P("shard"),
        P("shard"),
        P("shard", None),
        P("shard"),
        P("shard"),
        P("shard"),
        P("shard", None),
        P("shard"),
        P("shard", None),
        P("shard"),
    )
    out_specs = (
        P(("replica", "shard"), None),
        P(("replica", "shard"), None),
        P("shard"),
        P("shard"),
        P("shard", None),
        P("shard"),
        P("shard"),
        P("shard", None),
        P("shard"),
        P("shard"),
        P("shard"),
        P("shard", None),
        P("shard"),
        P("shard", None),
        P("shard"),
    )
    body = functools.partial(choose, mesh.shape["replica"], mesh.shape["shard"])
    return jax.shard_map(body, mesh=mesh, in_specs=in_specs, out_specs=out_specs, check_vma=False)
```

```python
import functools
import math

import jax
import jax.numpy as jnp
from jax import lax
from jax.experimental import pallas as pl
from jax.experimental.pallas import tpu as pltpu
from jax.sharding import PartitionSpec as P

HEADS = 16
HEAD_DIM = 64


EPSILON = 1e-05
TANH_SCALE = math.sqrt(2.0 / math.pi)
CUBIC = 0.044715


def product(left, right):
    return jnp.dot(left, right, preferred_element_type=jnp.float32)


def left_product(left, right):
    return lax.dot_general(
        left, right, (((0,), (0,)), ((), ())), preferred_element_type=jnp.float32
    )


def right_product(left, right):
    return lax.dot_general(
        left, right, (((1,), (1,)), ((), ())), preferred_element_type=jnp.float32
    )


def column_term(left, right):
    return left_product(left, right)


def gelu_parts(pre_act):
    inner_arg = TANH_SCALE * (pre_act + CUBIC * pre_act * pre_act * pre_act)
    tangent = jnp.tanh(inner_arg)
    gelu_value = 0.5 * pre_act * (1.0 + tangent)
    gelu_slope = 0.5 * (1.0 + tangent) + 0.5 * pre_act * (1.0 - tangent * tangent) * TANH_SCALE * (
        1.0 + 3.0 * CUBIC * pre_act * pre_act
    )
    return (gelu_value, gelu_slope)


def layer_norm(inputs, gain_row, bias_row):
    average = jnp.mean(inputs, axis=-1, keepdims=True)
    centred = inputs - average
    inv_std = lax.rsqrt(jnp.mean(centred * centred, axis=-1, keepdims=True) + EPSILON)
    normed = centred * inv_std
    return (normed * gain_row.astype(jnp.float32) + bias_row.astype(jnp.float32), normed, inv_std)


def norm_back(upstream, normed, inv_std, gain_row):
    scaled = upstream * gain_row.astype(jnp.float32)
    first_term = jnp.mean(scaled, axis=-1, keepdims=True)
    second_term = jnp.mean(scaled * normed, axis=-1, keepdims=True)
    input_grad = inv_std * (scaled - first_term - normed * second_term)
    return (input_grad, jnp.sum(upstream * normed, axis=0), jnp.sum(upstream, axis=0))


def seq_mask(lengths, row_count):
    seq_ends = jnp.cumsum(lengths, axis=-1)
    places = jnp.arange(row_count, dtype=jnp.int32)
    segment = jnp.sum((places[None, :, None] >= seq_ends[:, None, :]).astype(jnp.int32), axis=-1)
    causal = places[None, :] <= places[:, None]
    return (segment[:, :, None] == segment[:, None, :]) & causal[None]


def split_heads(flat_rows, groups):
    return flat_rows.reshape(groups, -1, flat_rows.shape[1] // HEAD_DIM, HEAD_DIM)


def attend_forward(queries, key_rows, values, allowed):
    groups = allowed.shape[0]
    scale_factor = 1.0 / math.sqrt(HEAD_DIM)
    head_q = split_heads(queries, groups)
    head_k = split_heads(key_rows, groups)
    head_v = split_heads(values, groups)
    scores = (
        jnp.einsum("gqhd,gkhd->ghqk", head_q, head_k, preferred_element_type=jnp.float32)
        * scale_factor
    )
    visible = allowed[:, None]
    row_total = jnp.sum(jnp.where(visible, jnp.exp(scores), 0.0), axis=-1, keepdims=True)
    log_total = jnp.log(row_total)
    probs_round = jnp.where(visible, jnp.exp(scores - log_total), 0.0).astype(jnp.bfloat16)
    context = jnp.einsum("ghqk,gkhd->gqhd", probs_round, head_v, preferred_element_type=jnp.float32)
    return (context.reshape(-1, queries.shape[1]).astype(jnp.bfloat16), log_total)


def attend_backward(queries, key_rows, values, allowed, log_total, context_grad):
    groups = allowed.shape[0]
    scale_factor = 1.0 / math.sqrt(HEAD_DIM)
    head_q = split_heads(queries, groups)
    head_k = split_heads(key_rows, groups)
    head_v = split_heads(values, groups)
    head_g = split_heads(context_grad, groups)
    scores = (
        jnp.einsum("gqhd,gkhd->ghqk", head_q, head_k, preferred_element_type=jnp.float32)
        * scale_factor
    )
    visible = allowed[:, None]
    exact_probs = jnp.where(visible, jnp.exp(scores - log_total), 0.0)
    probs_round = exact_probs.astype(jnp.bfloat16)
    prob_grad = jnp.einsum("gqhd,gkhd->ghqk", head_g, head_v, preferred_element_type=jnp.float32)
    value_grad = jnp.einsum(
        "ghqk,gqhd->gkhd", probs_round, head_g, preferred_element_type=jnp.float32
    )
    row_delta = jnp.sum(exact_probs * prob_grad, axis=-1, keepdims=True)
    score_grad = (exact_probs * (prob_grad - row_delta) * scale_factor).astype(jnp.bfloat16)
    query_grad = jnp.einsum(
        "ghqk,gkhd->gqhd", score_grad, head_k, preferred_element_type=jnp.float32
    )
    key_grad = jnp.einsum("ghqk,gqhd->gkhd", score_grad, head_q, preferred_element_type=jnp.float32)
    model_width = queries.shape[1]
    return (
        query_grad.reshape(-1, model_width),
        key_grad.reshape(-1, model_width),
        value_grad.reshape(-1, model_width),
    )


MESH = pl.DeviceIdType.MESH
VMEM_LIMIT = 60 * 1024 * 1024


def push(source, target, send_sem, recv_sem, device):
    return pltpu.make_async_remote_copy(
        src_ref=source,
        dst_ref=target,
        send_sem=send_sem,
        recv_sem=recv_sem,
        device_id=device,
        device_id_type=MESH,
    )


def greet(devices):
    barrier = pltpu.get_barrier_semaphore()
    for device in devices:
        pl.semaphore_signal(barrier, inc=1, device_id=device, device_id_type=MESH)
    pl.semaphore_wait(barrier, len(devices))


def group_peers(replica, me, size):
    return [(replica, lax.rem(me + k, size)) for k in range(1, size)]


class Spread:
    def __init__(self, blocks, replica, me, size, send, recv):
        core = lax.rem(me, 2)
        outer = me // 2
        half = size // 2
        self.partner = (replica, me + 1 - 2 * core)
        self.blocks, self.me, self.send, self.recv = blocks, me, send, recv
        self.size = size
        others = [lax.rem(outer + k, half) for k in range(1, half)]
        self.mates = [2 * j + core for j in others]
        self.far = [2 * j + 1 - core for j in others]
        self.replica = replica
        self.count = half

    def copy(self, k, block, device):
        return push(
            self.blocks.at[block], self.blocks.at[block], self.send.at[k], self.recv.at[block], device
        )

    def start(self):
        for k, mate in enumerate(self.mates):
            self.copy(k, self.me, (self.replica, mate)).start()
        self.copy(self.count, self.me, self.partner).start()

    def forward(self):
        for k, mate in enumerate(self.mates):
            self.copy(k, mate, self.partner).wait_recv()
            self.copy(self.count + 1 + k, mate, self.partner).start()

    def finish(self):
        for block in [self.partner[1]] + self.far:
            self.copy(0, block, self.partner).wait_recv()
        for k in range(len(self.mates)):
            self.copy(k, self.me, self.partner).wait_send()
            self.copy(self.count + 1 + k, self.me, self.partner).wait_send()
        self.copy(self.count, self.me, self.partner).wait_send()


def opening_kernel(size, hid_ref, grad_ref, par_ref, qkv_ref, up_ref,
                   hid_out, grad_out, par_out, qkv_out, up_out,
                   g_send, g_recv, w_send, w_recv, f_send, local_sem):
    replica = lax.axis_index("replica")
    me = lax.axis_index("shard")
    twin = replica + 1 - 2 * lax.rem(replica, 2)
    part = lax.rem(replica, 2)
    core = lax.rem(me, 2)
    outer = me // 2
    half = size // 2
    partner = me + 1 - 2 * core
    greet(group_peers(replica, me, size) + [(twin, me)])
    own = []
    for i, (src, dst) in enumerate(
        ((hid_ref, hid_out), (grad_ref, grad_out), (par_ref, par_out), (qkv_ref, qkv_out), (up_ref, up_out))
    ):
        if i < 3:
            own.append(pltpu.make_async_copy(src.at[0], dst.at[me], local_sem.at[i]))
        else:
            own.append(pltpu.make_async_copy(src.at[me], dst.at[me], local_sem.at[i]))
        own[-1].start()
    spreads = [
        Spread(out, replica, me, size, g_send.at[i], g_recv.at[i])
        for i, out in enumerate((hid_out, grad_out, par_out))
    ]
    own[0].wait()
    own[2].wait()
    spreads[2].start()
    spreads[0].start()
    remote = []
    for k in range(1, half):
        j = lax.rem(outer + k, half)
        remote += [2 * j + core, 2 * j + 1 - core]
    weights = ((qkv_ref, qkv_out), (up_ref, up_out))
    first = []
    for w, (src, dst) in enumerate(weights):
        for t, target in enumerate(remote):
            copy = push(
                src.at[target, part], dst.at[me, part],
                w_send.at[w, t], w_recv.at[w, me, part], (replica, target),
            )
            copy.start()
            first.append(copy)
        for h in range(2):
            copy = push(
                src.at[partner, h], dst.at[me, h],
                w_send.at[w, len(remote) + h], w_recv.at[w, me, h], (replica, partner),
            )
            copy.start()
            first.append(copy)
    own[1].wait()
    spreads[1].start()
    spreads[2].forward()
    spreads[0].forward()
    second = []
    for w, (src, dst) in enumerate(weights):
        for t, source in enumerate(remote):
            arrived = push(
                src.at[source, part], dst.at[source, part],
                w_send.at[w, t], w_recv.at[w, source, part], (replica, source),
            )
            arrived.wait_recv()
            copy = push(
                dst.at[source, part], dst.at[source, part],
                f_send.at[w, t], w_recv.at[w, source, part], (twin, me),
            )
            copy.start()
            second.append(copy)
    spreads[1].forward()
    for w, (src, dst) in enumerate(weights):
        for source in remote:
            push(
                dst.at[source, 1 - part], dst.at[source, 1 - part],
                f_send.at[w, 0], w_recv.at[w, source, 1 - part], (twin, me),
            ).wait_recv()
        for h in range(2):
            push(
                src.at[partner, h], dst.at[partner, h],
                w_send.at[w, 0], w_recv.at[w, partner, h], (replica, partner),
            ).wait_recv()
    for copy in first + second:
        copy.wait_send()
    own[3].wait()
    own[4].wait()
    for spread in spreads:
        spread.finish()


def vmem_specs(count):
    return [pl.BlockSpec(memory_space=pltpu.VMEM)] * count


def opening(size, hidden, upstream, params, qkv_parts, up_parts):
    dma = pltpu.SemaphoreType.DMA
    shape = lambda array: jax.ShapeDtypeStruct((size,) + array.shape[1:], array.dtype)
    arrays = (hidden[None], upstream[None], params[None], qkv_parts, up_parts)
    return pl.pallas_call(
        functools.partial(opening_kernel, size),
        out_shape=tuple(shape(a) for a in arrays),
        in_specs=vmem_specs(5),
        out_specs=tuple(vmem_specs(5)),
        scratch_shapes=[
            dma((3, size)), dma((3, size)), dma((2, size)), dma((2, size, 2)), dma((2, size)), dma((5,)),
        ],
        compiler_params=pltpu.CompilerParams(
            collective_id=0, has_side_effects=True, vmem_limit_bytes=VMEM_LIMIT
        ),
    )(*arrays)


def group_sum_kernel(size, gathers, *refs):
    n = len(gathers)
    half = size // 2
    ins, outs = refs[:n], refs[n : 2 * n]
    scratch = refs[2 * n :]
    replica = lax.axis_index("replica")
    me = lax.axis_index("shard")
    core = lax.rem(me, 2)
    outer = me // 2
    partner = (replica, me + 1 - 2 * core)
    greet(group_peers(replica, me, size))
    order = [lax.rem(outer + k, half) for k in range(1, half)] + [outer]
    work = []
    for i in range(n):
        near, summed, far, p_send, p_recv, x_send, x_recv, g_send, g_recv = scratch[9 * i : 9 * i + 9]
        for k, j in enumerate(order):
            push(
                ins[i].at[2 * j + 1 - core], near.at[j], p_send.at[k], p_recv.at[j], partner
            ).start()
    for i in range(n):
        near, summed, far, p_send, p_recv, x_send, x_recv, g_send, g_recv = scratch[9 * i : 9 * i + 9]
        for k, j in enumerate(order):
            push(ins[i].at[2 * j + 1 - core], near.at[j], p_send.at[k], p_recv.at[j], partner).wait_recv()
            if k < half - 1:
                block = ins[i][2 * j + core].astype(jnp.float32) + near[j].astype(jnp.float32)
                summed[k] = block.astype(jnp.bfloat16)
                push(
                    summed.at[k], far.at[outer], x_send.at[k], x_recv.at[outer], (replica, 2 * j + core)
                ).start()
    spreads = []
    for i in range(n):
        near, summed, far, p_send, p_recv, x_send, x_recv, g_send, g_recv = scratch[9 * i : 9 * i + 9]
        total = ins[i][me].astype(jnp.float32) + near[outer].astype(jnp.float32)
        for k, j in enumerate(order[:-1]):
            push(
                summed.at[k], far.at[j], x_send.at[k], x_recv.at[j], (replica, 2 * j + core)
            ).wait_recv()
            total = total + far[j].astype(jnp.float32)
        if gathers[i]:
            outs[i][me] = total.astype(outs[i].dtype)
            spread = Spread(outs[i], replica, me, size, g_send, g_recv)
            spread.start()
            spreads.append(spread)
        else:
            outs[i][...] = total.astype(outs[i].dtype)
    for spread in spreads:
        spread.forward()
    for spread in spreads:
        spread.finish()
    for i in range(n):
        near, summed, far, p_send, p_recv, x_send, x_recv, g_send, g_recv = scratch[9 * i : 9 * i + 9]
        for k, j in enumerate(order):
            push(ins[i].at[2 * j + 1 - core], near.at[j], p_send.at[k], p_recv.at[j], partner).wait_send()
            if k < half - 1:
                push(
                    summed.at[k], far.at[outer], x_send.at[k], x_recv.at[outer], (replica, 2 * j + core)
                ).wait_send()


def group_sum(size, partials, gathers, collective):
    dma = pltpu.SemaphoreType.DMA
    half = size // 2
    shapes, scratch, blocks = [], [], []
    for partial, gather in zip(partials, gathers):
        block = partial.reshape(size, -1, partial.shape[-1])
        blocks.append(block)
        if gather:
            shapes.append(jax.ShapeDtypeStruct(block.shape, jnp.bfloat16))
        else:
            shapes.append(jax.ShapeDtypeStruct(block.shape[1:], jnp.float32))
        for _ in range(3):
            scratch.append(pltpu.VMEM((half,) + block.shape[1:], jnp.bfloat16))
        scratch += [dma((half,)), dma((half,)), dma((half,)), dma((half,)), dma((size,)), dma((size,))]
    return pl.pallas_call(
        functools.partial(group_sum_kernel, size, gathers),
        out_shape=tuple(shapes),
        in_specs=vmem_specs(len(blocks)),
        out_specs=tuple(vmem_specs(len(blocks))),
        scratch_shapes=scratch,
        compiler_params=pltpu.CompilerParams(
            collective_id=collective, has_side_effects=True, vmem_limit_bytes=VMEM_LIMIT
        ),
    )(*blocks)


KEEP, SWAP, ADD = 0, 1, 2


def closing_kernel(size, ring, modes, *refs):
    n = len(modes)
    ins, outs, lands = refs[:n], refs[n : 2 * n], refs[2 * n : 3 * n]
    swaps = refs[3 * n : 4 * n]
    r_send, r_recv, a_send, a_recv, s_send, s_recv = refs[4 * n :]
    replica = lax.axis_index("replica")
    me = lax.axis_index("shard")
    side = lax.rem(replica, 2)
    depth = replica // 2
    place = (1 - side) * depth + side * (ring - 1 - depth)
    step = 1 - 2 * lax.rem(me, 2)

    def member(position):
        position = lax.rem(position + 2 * ring, ring)
        late = position // (ring // 2)
        return (1 - late) * 2 * position + late * (2 * (ring - 1 - position) + 1)

    after = (member(place + step), me)
    before = (member(place - step), me)
    chunk = lambda hops: lax.rem(place - step * hops + 2 * ring, ring)
    greet(group_peers(replica, me, size) + [after, before])

    def reduce_copy(i, k):
        source = ins[i].at[chunk(1)] if k == 0 else lands[i].at[k - 1]
        return push(source, lands[i].at[k], r_send.at[i, k], r_recv.at[i, k], after)

    for i in range(n):
        reduce_copy(i, 0).start()
    for k in range(ring - 1):
        for i in range(n):
            reduce_copy(i, k).wait_recv()
            mine = ins[i][chunk(k + 2)].astype(jnp.float32)
            total = (mine + lands[i][k].astype(jnp.float32)).astype(lands[i].dtype)
            lands[i][k] = total
            if k < ring - 2:
                reduce_copy(i, k + 1).start()
            elif modes[i] == KEEP:
                outs[i][place] = total

    def swap_copy(i, k, source):
        target = lax.rem(me + k, size)
        return push(
            lands[i].at[ring - 2, target], swaps[i].at[source],
            s_send.at[i, k], s_recv.at[i, source], (replica, target),
        )

    for i in range(n):
        if modes[i] != KEEP:
            for k in range(1, size):
                swap_copy(i, k, me).start()
            swaps[i][me] = lands[i][ring - 2, me]

    def gather_copy(i, k):
        return push(
            outs[i].at[chunk(k)], outs[i].at[chunk(k)], a_send.at[i, k], a_recv.at[i, k], after
        )

    def arrival(i, k):
        return push(
            outs[i].at[chunk(k + 1)], outs[i].at[chunk(k + 1)], a_send.at[i, k], a_recv.at[i, k], after
        )

    order = [i for i in range(n) if modes[i] == KEEP] + [i for i in range(n) if modes[i] != KEEP]
    for i in order:
        if modes[i] != KEEP:
            for k in range(1, size):
                swap_copy(i, size - k, lax.rem(me + k, size)).wait_recv()
            if modes[i] == SWAP:
                outs[i][place] = swaps[i][...]
            else:
                outs[i][place] = jnp.sum(swaps[i][...], axis=0)
        gather_copy(i, 0).start()
    for k in range(ring - 1):
        for i in order:
            arrival(i, k).wait_recv()
            if k < ring - 2:
                gather_copy(i, k + 1).start()
    for i in range(n):
        for k in range(ring - 1):
            reduce_copy(i, k).wait_send()
            gather_copy(i, k).wait_send()
        if modes[i] != KEEP:
            for k in range(1, size):
                swap_copy(i, k, me).wait_send()


def closing(size, ring, arrays, modes):
    dma = pltpu.SemaphoreType.DMA
    n = len(arrays)
    shapes, lands, swaps = [], [], []
    for array, mode in zip(arrays, modes):
        out = array.shape if mode != ADD else array.shape[:1] + array.shape[2:]
        shapes.append(jax.ShapeDtypeStruct(out, array.dtype))
        lands.append(pltpu.VMEM((ring - 1,) + array.shape[1:], array.dtype))
        swaps.append(
            pltpu.VMEM(array.shape[1:] if mode != KEEP else (8, 128), array.dtype)
        )
    return pl.pallas_call(
        functools.partial(closing_kernel, size, ring, modes),
        out_shape=tuple(shapes),
        in_specs=vmem_specs(n),
        out_specs=tuple(vmem_specs(n)),
        scratch_shapes=lands + swaps + [
            dma((n, ring)), dma((n, ring)), dma((n, ring)), dma((n, ring)), dma((n, size)), dma((n, size)),
        ],
        compiler_params=pltpu.CompilerParams(
            collective_id=5, has_side_effects=True, vmem_limit_bytes=VMEM_LIMIT
        ),
    )(*arrays)


def local(
    ring,
    size,
    hidden_in,
    out_grad,
    lengths,
    norm1_gain,
    norm1_bias,
    qkv_weight,
    query_bias,
    value_bias,
    out_weight,
    out_bias,
    norm2_gain,
    norm2_bias,
    up_weight,
    up_bias,
    down_weight,
    down_bias,
):
    me = lax.axis_index("shard")
    rows, width = hidden_in.shape
    band = width // size
    seqs = lengths.shape[1]
    lane_count = max(band, 128)
    wide = lambda vector: jnp.pad(vector, (0, lane_count - vector.shape[0]))
    params = jnp.stack(
        [
            wide(v)
            for v in (
                norm1_gain, norm1_bias, out_bias, norm2_gain, norm2_bias, down_bias,
                lengths[0].astype(jnp.bfloat16), norm1_gain,
            )
        ]
    )
    qkv_parts = qkv_weight.reshape(2, band // 2, 3, size, band).transpose(3, 0, 1, 2, 4)
    qkv_parts = qkv_parts.reshape(size, 2, band // 2, 3 * band)
    ff_band = up_weight.shape[1] // size
    up_parts = up_weight.reshape(2, band // 2, size, ff_band).transpose(2, 0, 1, 3)
    hidden_all, upstream_all, params_all, qkv_all, up_all = opening(
        size, hidden_in, out_grad, params, qkv_parts, up_parts
    )
    hidden_all = hidden_all.reshape(size * rows, width)
    grad_all = upstream_all.reshape(size * rows, width)
    qkv_cols = qkv_all.reshape(width, 3 * band)
    up_cols = up_all.reshape(width, ff_band)
    gain_one, bias_one, outb_full, gain_two, bias_two, downb_full = (
        params_all[:, i, :band].reshape(width) for i in range(6)
    )
    lengths_all = params_all[:, 6, :seqs].astype(jnp.int32)
    mine = lambda array: lax.dynamic_slice_in_dim(array, me * band, band, axis=array.ndim - 1)
    own_rows = lambda array: lax.dynamic_slice_in_dim(array, me * rows, rows, axis=0)

    allowed = seq_mask(lengths_all, rows)
    inputs_wide = hidden_all.astype(jnp.float32)
    first_out, normed_one, inv_one = layer_norm(inputs_wide, gain_one, bias_one)
    first_in = first_out.astype(jnp.bfloat16)
    projected = product(first_in, qkv_cols)
    queries = (projected[:, :band] + query_bias.astype(jnp.float32)).astype(jnp.bfloat16)
    key_rows = projected[:, band : 2 * band].astype(jnp.bfloat16)
    values = (projected[:, 2 * band :] + value_bias.astype(jnp.float32)).astype(jnp.bfloat16)
    context, log_total = attend_forward(queries, key_rows, values, allowed)
    (attended,) = group_sum(
        size, [product(context, out_weight).astype(jnp.bfloat16)], (True,), 1
    )
    residual = (
        inputs_wide
        + attended.reshape(size * rows, width).astype(jnp.float32)
        + outb_full.astype(jnp.float32)
    )
    second_out, normed_two, inv_two = layer_norm(residual, gain_two, bias_two)
    second_in = second_out.astype(jnp.bfloat16)
    pre_act = product(second_in, up_cols) + up_bias.astype(jnp.float32)
    activ_value, gelu_slope = gelu_parts(pre_act)
    activated = activ_value.astype(jnp.bfloat16)
    down_part = product(activated, down_weight).astype(jnp.bfloat16)
    upstream = grad_all.astype(jnp.float32)
    pre_grad = right_product(grad_all, down_weight) * gelu_slope
    pre_round = pre_grad.astype(jnp.bfloat16)
    second_part = right_product(pre_round, up_cols).astype(jnp.bfloat16)
    second_sum, down_sum = group_sum(size, [second_part, down_part], (True, False), 2)
    hidden_out = (own_rows(residual) + down_sum + downb_full.astype(jnp.float32)).astype(
        jnp.bfloat16
    )
    down_grad = column_term(activated, grad_all).astype(jnp.bfloat16)
    up_grad = column_term(second_in, pre_round).astype(jnp.bfloat16)
    second_grad = second_sum.reshape(size * rows, width).astype(jnp.float32)
    norm_two_in, gain2_grad, bias2_grad = norm_back(second_grad, normed_two, inv_two, gain_two)
    resid_grad = upstream + norm_two_in
    resid_round = resid_grad.astype(jnp.bfloat16)
    outw_grad = column_term(context, resid_round).astype(jnp.bfloat16)
    context_grad = right_product(resid_round, out_weight).astype(jnp.bfloat16)
    query_grad, key_grad, value_grad = attend_backward(
        queries, key_rows, values, allowed, log_total, context_grad
    )
    qkv_grad = jnp.concatenate([query_grad, key_grad, value_grad], axis=1).astype(jnp.bfloat16)
    first_part = right_product(qkv_grad, qkv_cols).astype(jnp.bfloat16)
    (first_grad,) = group_sum(size, [first_part], (False,), 3)
    qkvw_grad = column_term(first_in, qkv_grad).astype(jnp.bfloat16)
    norm_one_in, gain1_grad, bias1_grad = norm_back(
        first_grad, own_rows(normed_one), own_rows(inv_one), gain_one
    )
    in_grad = (own_rows(resid_grad) + norm_one_in).astype(jnp.bfloat16)

    owned = jnp.concatenate(
        [
            jnp.sum(query_grad, axis=0),
            jnp.sum(value_grad, axis=0),
            mine(jnp.sum(resid_grad, axis=0)),
            mine(gain2_grad),
            mine(bias2_grad),
            jnp.sum(pre_grad, axis=0),
            mine(jnp.sum(upstream, axis=0)),
        ]
    )
    here = (jnp.arange(size) == me)[:, None]
    small = jnp.concatenate(
        [
            gain1_grad.reshape(size, band),
            bias1_grad.reshape(size, band),
            jnp.where(here, owned[None], 0.0),
        ],
        axis=1,
    )
    count = small.shape[1]
    small = small.reshape(size, ring, 1, count // ring).transpose(1, 0, 2, 3)
    slab = band // ring
    by_owner = lambda array: array.reshape(size, ring, slab, array.shape[1]).transpose(1, 0, 2, 3)
    down_all, outw_all, up_total, qkv_total, small_all = closing(
        size,
        ring,
        [
            down_grad.reshape(ring, -1, width),
            outw_grad.reshape(ring, -1, width),
            by_owner(up_grad),
            by_owner(qkvw_grad),
            small,
        ],
        (KEEP, KEEP, SWAP, SWAP, ADD),
    )
    downw_total = down_all.reshape(down_weight.shape).astype(jnp.float32)
    outw_total = outw_all.reshape(out_weight.shape).astype(jnp.float32)
    upw_total = up_total.transpose(0, 2, 1, 3).reshape(up_weight.shape).astype(jnp.float32)
    qkvw_total = (
        qkv_total.reshape(ring, size, slab, 3, band)
        .transpose(0, 2, 3, 1, 4)
        .reshape(qkv_weight.shape)
        .astype(jnp.float32)
    )
    flat = small_all.reshape(count)
    pieces = []
    offset = 0
    for length in (band, band, band, band, band, band, band, ff_band, band):
        pieces.append(flat[offset : offset + length])
        offset += length
    gain1_t, bias1_t, qbias_t, vbias_t, outb_t, gain2_t, bias2_t, upb_t, downb_t = pieces
    return (
        hidden_out,
        in_grad,
        gain1_t,
        bias1_t,
        qkvw_total,
        qbias_t,
        vbias_t,
        outw_total,
        outb_t,
        gain2_t,
        bias2_t,
        upw_total,
        upb_t,
        downw_total,
        downb_t,
    )


def lanes(start, width):
    return pl.ds(pl.multiple_of(start, 128), width)


def entry_kernel(size, splits, hid_ref, grad_ref, par_ref, qkv_ref, up_ref,
                 hid_out, grad_out, par_out, qkv_out, up_out,
                 g_send, g_recv, w_send, w_recv, f_send, local_sem, own_sem):
    replica = lax.axis_index("replica")
    me = lax.axis_index("shard")
    low = lax.rem(replica, 2)
    high = lax.rem(replica // 2, 2)
    part = low + 2 * high
    core = lax.rem(me, 2)
    outer = me // 2
    half = size // 2
    partner = me + 1 - 2 * core
    flips = ((1, 0), (0, 1), (1, 1))
    twins = [replica + a * (1 - 2 * low) + 2 * b * (1 - 2 * high) for a, b in flips]
    theirs = [
        (low + a * (1 - 2 * low)) + 2 * (high + b * (1 - 2 * high)) for a, b in flips
    ]
    weights = ((qkv_ref, qkv_out), (up_ref, up_out))
    own = []
    for i, (src, dst) in enumerate(((hid_ref, hid_out), (grad_ref, grad_out), (par_ref, par_out))):
        own.append(pltpu.make_async_copy(src.at[0], dst.at[me], local_sem.at[i]))
        own[-1].start()

    def views(w, owner, target, which):
        src, dst = weights[w]
        span = src.shape[2] // splits[w]
        wide = span // size
        for j in range(splits[w]):
            yield (
                j,
                src.at[which, :, lanes(j * span + target * wide, wide)],
                dst.at[owner, which, :, pl.ds(j * wide, wide)],
            )

    full = slice(None)
    for w in range(2):
        for j, source, target in views(w, me, me, full):
            own.append(pltpu.make_async_copy(source, target, own_sem.at[w, j]))
            own[-1].start()
    greet(group_peers(replica, me, size) + [(twin, me) for twin in twins])
    spreads = [
        Spread(out, replica, me, size, g_send.at[i], g_recv.at[i])
        for i, out in enumerate((hid_out, grad_out, par_out))
    ]
    remote = []
    for k in range(1, half):
        j = lax.rem(outer + k, half)
        remote += [2 * j + core, 2 * j + 1 - core]
    first = []
    for w in range(2):
        for t, target in enumerate(remote):
            for j, source, landing in views(w, me, target, part):
                copy = push(
                    source, landing, w_send.at[w, t, j], w_recv.at[w, me, part, j], (replica, target)
                )
                copy.start()
                first.append(copy)
        for j, source, landing in views(w, me, partner, full):
            copy = push(
                source, landing, w_send.at[w, len(remote), j], w_recv.at[w, me, 0, j],
                (replica, partner),
            )
            copy.start()
            first.append(copy)
    for i in (2, 0, 1):
        own[i].wait()
        spreads[i].start()
    second = []
    for w in range(2):
        dst = weights[w][1]
        for t, source in enumerate(remote):
            for j, view, landing in views(w, source, me, part):
                push(
                    view, landing, w_send.at[w, t, j], w_recv.at[w, source, part, j], (replica, source)
                ).wait_recv()
            for m, twin in enumerate(twins):
                copy = push(
                    dst.at[source, part], dst.at[source, part],
                    f_send.at[w, t, m], w_recv.at[w, source, part, 0], (twin, me),
                )
                copy.start()
                second.append(copy)
    for i in (2, 0, 1):
        spreads[i].forward()
    for w in range(2):
        dst = weights[w][1]
        for source in remote:
            for m, twin in enumerate(twins):
                push(
                    dst.at[source, theirs[m]], dst.at[source, theirs[m]],
                    f_send.at[w, 0, m], w_recv.at[w, source, theirs[m], 0], (twin, me),
                ).wait_recv()
        for j, view, landing in views(w, partner, me, full):
            push(
                view, landing, w_send.at[w, 0, j], w_recv.at[w, partner, 0, j], (replica, partner)
            ).wait_recv()
    for copy in first + second:
        copy.wait_send()
    for copy in own[3:]:
        copy.wait()
    for spread in spreads:
        spread.finish()


def entry(size, hidden, upstream, params, qkv_weight, up_weight):
    dma = pltpu.SemaphoreType.DMA
    band = qkv_weight.shape[0]
    shape = lambda array: jax.ShapeDtypeStruct((size,) + array.shape[1:], array.dtype)
    gathers = (hidden[None], upstream[None], params[None])
    weights = tuple(w.reshape(4, band // 4, w.shape[1]) for w in (qkv_weight, up_weight))
    outs = tuple(shape(a) for a in gathers) + tuple(
        jax.ShapeDtypeStruct((size, 4, band // 4, w.shape[2] // size), w.dtype) for w in weights
    )
    return pl.pallas_call(
        functools.partial(entry_kernel, size, (3, 1)),
        out_shape=outs,
        in_specs=[pl.BlockSpec(memory_space=pl.ANY)] * 5,
        out_specs=tuple(vmem_specs(5)),
        scratch_shapes=[
            dma((3, size)), dma((3, size)), dma((2, size, 3)), dma((2, size, 4, 3)),
            dma((2, size, 3)), dma((3,)), dma((2, 3)),
        ],
        compiler_params=pltpu.CompilerParams(
            collective_id=0, has_side_effects=True, vmem_limit_bytes=VMEM_LIMIT
        ),
    )(*gathers, *weights)


class Where:
    def __init__(self, size, ring):
        self.size, self.ring = size, ring
        self.replica = lax.axis_index("replica")
        self.me = lax.axis_index("shard")
        self.core = lax.rem(self.me, 2)
        self.outer = self.me // 2
        self.half = size // 2
        self.partner = (self.replica, self.me + 1 - 2 * self.core)
        self.order = [lax.rem(self.outer + k, self.half) for k in range(1, self.half)] + [self.outer]
        side = lax.rem(self.replica, 2)
        depth = self.replica // 2
        self.place = (1 - side) * depth + side * (ring - 1 - depth)
        self.step = 1 - 2 * self.core
        self.after = (self.member(self.place + self.step), self.me)
        self.before = (self.member(self.place - self.step), self.me)

    def member(self, position):
        ring = self.ring
        position = lax.rem(position + 2 * ring, ring)
        late = position // (ring // 2)
        return (1 - late) * 2 * position + late * (2 * (ring - 1 - position) + 1)

    def chunk(self, hops):
        return lax.rem(self.place - self.step * hops + 2 * self.ring, self.ring)


class Ring:
    def __init__(self, where, i, source, land, out, swap, sems, mode, pieces=1):
        self.where, self.source, self.land, self.out, self.swap = where, source, land, out, swap
        self.r_send, self.r_recv, self.a_send, self.a_recv, self.s_send, self.s_recv = (
            sem.at[i] for sem in sems
        )
        self.mode, self.pieces = mode, pieces
        self.last = where.ring - 2

    def block(self, position):
        return self.source.at[:, position] if self.mode == SWAP else self.source.at[position]

    def reduce_copy(self, k):
        source = self.block(self.where.chunk(1)) if k == 0 else self.land.at[k - 1]
        return push(source, self.land.at[k], self.r_send.at[k], self.r_recv.at[k], self.where.after)

    def swap_copy(self, k, source):
        where = self.where
        target = lax.rem(where.me + k, where.size)
        return push(
            self.land.at[self.last, target], self.swap.at[source],
            self.s_send.at[k], self.s_recv.at[source], (where.replica, target),
        )

    def gather_copy(self, k, hops):
        part = self.spot(self.where.chunk(hops))
        return push(part, part, self.a_send.at[k], self.a_recv.at[k], self.where.after)

    def spot(self, position):
        if self.mode != ADD:
            return self.out.at[position]
        wide = self.land.shape[-1]
        return self.out.at[:, lanes(position * wide, wide)]

    def start(self):
        self.reduce_copy(0).start()

    def reduce_step(self, k):
        where, land = self.where, self.land
        self.reduce_copy(k).wait_recv()
        position = where.chunk(k + 2)
        mine = self.source[:, position] if self.mode == SWAP else self.source[position]
        total = (mine.astype(ADDS) + land[k].astype(ADDS)).astype(land.dtype)
        land[k] = total
        if k < self.last:
            self.reduce_copy(k + 1).start()
        elif self.mode == KEEP:
            self.out[where.place] = total
            self.gather_copy(0, 0).start()
        else:
            for step in range(1, where.size):
                self.swap_copy(step, where.me).start()
            self.swap[where.me] = land[k, where.me]

    def turn(self):
        where = self.where
        if self.mode == KEEP:
            return
        for k in range(1, where.size):
            self.swap_copy(where.size - k, lax.rem(where.me + k, where.size)).wait_recv()
        if self.mode == ADD:
            self.spot(where.place)[...] = jnp.sum(self.swap[...], axis=0)
        else:
            wide = self.land.shape[-1] // self.pieces
            for s in range(where.size):
                for j in range(self.pieces):
                    start = (j * where.size + s) * wide
                    self.out[where.place, :, start : start + wide] = self.swap[
                        s, :, j * wide : (j + 1) * wide
                    ]
        self.gather_copy(0, 0).start()

    def gather_step(self, k):
        self.gather_copy(k, k + 1).wait_recv()
        if k < self.last:
            self.gather_copy(k + 1, k + 1).start()

    def stages(self):
        steps = [functools.partial(self.reduce_step, k) for k in range(self.last + 1)]
        if self.mode != KEEP:
            steps.append(self.turn)
        return steps + [functools.partial(self.gather_step, k) for k in range(self.last + 1)]

    def drain(self):
        for k in range(self.last + 1):
            self.reduce_copy(k).wait_send()
            self.gather_copy(k, k).wait_send()
        if self.mode != KEEP:
            for k in range(1, self.where.size):
                self.swap_copy(k, self.where.me).wait_send()


class GroupSum:
    def __init__(self, where, source, near, summed, far, sems):
        self.where, self.source, self.near, self.summed, self.far = where, source, near, summed, far
        self.p_send, self.p_recv, self.x_send, self.x_recv = sems

    def near_copy(self, k):
        j = self.where.order[k]
        return push(
            self.source.at[2 * j + 1 - self.where.core], self.near.at[j],
            self.p_send.at[k], self.p_recv.at[j], self.where.partner,
        )

    def far_copy(self, k, landing):
        where = self.where
        return push(
            self.summed.at[k], self.far.at[landing], self.x_send.at[k], self.x_recv.at[landing],
            (where.replica, 2 * where.order[k] + where.core),
        )

    def send(self, k):
        self.near_copy(k).start()

    def reduce(self, k):
        where = self.where
        j = where.order[k]
        self.near_copy(k).wait_recv()
        block = self.source[2 * j + where.core].astype(jnp.float32) + self.near[j].astype(jnp.float32)
        self.summed[k] = block.astype(jnp.bfloat16)
        self.far_copy(k, where.outer).start()

    def arrive(self):
        self.near_copy(self.where.half - 1).wait_recv()
        for k in range(self.where.half - 1):
            self.far_copy(k, self.where.order[k]).wait_recv()

    def tile(self, rows):
        where = self.where
        total = self.source[where.me, rows].astype(jnp.float32) + self.near[
            where.outer, rows
        ].astype(jnp.float32)
        for j in where.order[:-1]:
            total = total + self.far[j, rows].astype(jnp.float32)
        return total

    def drain(self):
        for k in range(self.where.half):
            self.near_copy(k).wait_send()
            if k < self.where.half - 1:
                self.far_copy(k, self.where.outer).wait_send()


TILE = 16
PAIR_SERVE = 0
SPLIT = 2
ADDS = jnp.float32
LATE_RATE = 1


def tiles(count, body):
    @pl.loop(0, count // TILE)
    def _(t):
        body(pl.ds(pl.multiple_of(t * TILE, TILE), TILE))


def fold(value):
    return jnp.sum(value.reshape(TILE // 8, 8, value.shape[-1]), axis=0)


def row_stats(inputs):
    average = jnp.mean(inputs, axis=-1, keepdims=True)
    centred = inputs - average
    inv_std = lax.rsqrt(jnp.mean(centred * centred, axis=-1, keepdims=True) + EPSILON)
    return (centred * inv_std, inv_std)


def row_back(upstream, normed, inv_std, gain_row):
    scaled = upstream * gain_row
    first_term = jnp.mean(scaled, axis=-1, keepdims=True)
    second_term = jnp.mean(scaled * normed, axis=-1, keepdims=True)
    return inv_std * (scaled - first_term - normed * second_term)


def back_kernel(size, ring,
                act_ref, pre_ref, grad_ref, vec_ref, upb_ref,
                sec_hbm, upw_hbm, dnw_hbm, resid_hbm, hid_hbm,
                q_hbm, k_hbm, v_hbm, allow_hbm, ctx_hbm, outw_hbm, first_hbm, qkvw_hbm,
                hidden_out, in_out, down_out, outw_out, up_out, qkv_out, small_out,
                sec_ref, upw_ref, dnw_ref, resid_ref, hid_ref,
                q_ref, k_ref, v_ref, allow_ref, ctx_ref, outw_ref, first_ref, qkvw_ref,
                second_ref, down_ref, dgrad_ref, ugrad_ref, load_sem,
                near_a, summed_a, far_a, near_b, summed_b, far_b, near_c, summed_c, far_c,
                ssum, fpart, rgrad, rround, qkvg, outg, qkvwg, small, acc, bias,
                land_d, land_o, land_u, land_q, land_s, swap_u, swap_q, swap_s,
                p_send, p_recv, x_send, x_recv, g_send, g_recv,
                r_send, r_recv, a_send, a_recv, s_send, s_recv):
    where = Where(size, ring)
    me, replica = where.me, where.replica
    rows, width = hid_ref.shape
    band = q_ref.shape[2]
    slab = band // ring
    scale_factor = 1.0 / math.sqrt(HEAD_DIM)
    loads = [
        pltpu.make_async_copy(source, target, load_sem.at[i])
        for i, (source, target) in enumerate(
            (
                (sec_hbm, sec_ref), (upw_hbm, upw_ref), (resid_hbm, resid_ref), (dnw_hbm, dnw_ref),
                (ctx_hbm, ctx_ref), (outw_hbm, outw_ref), (q_hbm, q_ref), (k_hbm, k_ref),
                (v_hbm, v_ref), (allow_hbm, allow_ref), (qkvw_hbm, qkvw_ref), (first_hbm, first_ref),
                (hid_hbm, hid_ref),
            )
        )
    ]
    for load in loads:
        load.start()
    greet(group_peers(replica, me, size) + [where.after, where.before])
    flat = lambda value: value.reshape(size * rows, value.shape[-1])
    sems = (r_send, r_recv, a_send, a_recv, s_send, s_recv)
    index = iter(range(r_send.shape[0]))

    def rings(source, land, out, swap, mode, count, pieces=1):
        made = []
        deep = out.shape[1] // count
        for n in range(count):
            part = pl.ds(n * deep, deep)
            views = (
                (source.at[:, part], land.at[:, part], out.at[:, part], None)
                if mode == KEEP
                else (source.at[:, :, part], land.at[:, :, part], out.at[:, part], swap.at[:, part])
            )
            made.append(Ring(where, next(index), *views, sems, mode, pieces))
        return made

    down_rings = rings(dgrad_ref, land_d, down_out, None, KEEP, SPLIT)
    up_rings = rings(ugrad_ref, land_u, up_out, swap_u, SWAP, SPLIT)
    outw_rings = rings(outg, land_o, outw_out, None, KEEP, 1)
    qkv_rings = rings(qkvwg, land_q, qkv_out, swap_q, SWAP, SPLIT, 3)
    small_ring = Ring(where, next(index), small, land_s, small_out, swap_s, sems, ADD)
    all_rings = down_rings + up_rings + outw_rings + qkv_rings + [small_ring]

    def launch(made):
        for ring_ in made:
            ring_.start()

    def woven(queues):
        queues = [list(queue) for queue in queues]
        order = []
        while any(queues):
            for queue in queues:
                if queue:
                    order.append(queue.pop(0))
        return order

    stages_of = lambda made: [ring_.stages() for ring_ in made]
    sums = []
    for i, buffers in enumerate(
        (
            (second_ref, near_a, summed_a, far_a),
            (down_ref, near_b, summed_b, far_b),
            (fpart, near_c, summed_c, far_c),
        )
    ):
        sums.append(
            GroupSum(where, *buffers, (p_send.at[i], p_recv.at[i], x_send.at[i], x_recv.at[i]))
        )
    second_sum, down_sum, first_sum = sums
    half = where.half

    deep = dgrad_ref.shape[1]

    def down_chunk(hops):
        position = where.chunk(hops)
        grad = left_product(act_ref[:, lanes(position * deep, deep)], flat(grad_ref[...]))
        dgrad_ref[position] = grad.astype(jnp.bfloat16)

    def own_rows(block):
        return pl.ds(pl.multiple_of(block * rows, rows), rows)

    def second_block(block):
        grad = right_product(pre_ref[own_rows(block)], upw_ref[...])
        second_ref[block] = grad.astype(jnp.bfloat16)

    def down_block(block):
        part = product(act_ref[own_rows(block)], dnw_ref[...])
        down_ref[block] = part.astype(jnp.bfloat16)

    down_chunk(1)
    launch(down_rings)
    loads[0].wait()

    @pl.loop(0, size)
    def _(t):
        grad = left_product(sec_ref[:, lanes(t * band, band)], pre_ref[...])
        ugrad_ref[t] = grad.astype(jnp.bfloat16).reshape(ugrad_ref.shape[1:])

    launch(up_rings)
    loads[1].wait()
    for k in range(half):
        second_block(2 * where.order[k] + 1 - where.core)
        second_sum.send(k)

    @pl.loop(2, ring + 1)
    def _(hops):
        down_chunk(hops)

    for k in range(half):
        second_block(2 * where.order[k] + where.core)
    ffn_rings = [ring_ for pair in zip(down_rings, up_rings) for ring_ in pair]
    early = woven(stages_of(ffn_rings))

    def serve(count):
        for _ in range(count * SPLIT):
            if early:
                early.pop(0)()

    for k in range(half - 1):
        second_sum.reduce(k)
    acc[...] = jnp.zeros_like(acc)
    bias[...] = jnp.zeros_like(bias)
    small[...] = jnp.zeros_like(small)
    serve(2)
    second_sum.arrive()

    def second_total(part):
        ssum[me, part] = second_sum.tile(part).astype(jnp.bfloat16)

    tiles(rows, second_total)
    spread = Spread(ssum, replica, me, size, g_send, g_recv)
    spread.start()
    loads[2].wait()
    serve(1)

    def norm_two(block):
        def body(part):
            normed, inv_std = row_stats(resid_ref[block, part])
            upper = ssum[block, part].astype(jnp.float32)
            total = grad_ref[block, part].astype(jnp.float32) + row_back(
                upper, normed, inv_std, vec_ref[1:2]
            )
            rgrad[block, part] = total
            rround[block, part] = total.astype(jnp.bfloat16)
            acc[0] += fold(upper * normed)
            acc[1] += fold(upper)
            acc[2] += fold(total)

        tiles(rows, body)

    norm_two(me)
    serve(1)
    spread.forward()
    serve(1)
    spread.finish()
    for k in range(1, size):
        norm_two(lax.rem(me + k, size))
        serve(1)

    loads[4].wait()

    @pl.loop(0, width // 256)
    def _(t):
        cut = lanes(t * 256, 256)
        grad = left_product(flat(ctx_ref[...]), flat(rround[:, :, cut]))
        outg[:, :, cut] = grad.astype(jnp.bfloat16).reshape(ring, slab, 256)

    launch(outw_rings)
    loads[3].wait()
    for k in range(half):
        down_block(2 * where.order[k] + 1 - where.core)
        down_sum.send(k)
    for k in range(half):
        down_block(2 * where.order[k] + where.core)
    for k in range(half - 1):
        down_sum.reduce(k)
    outw_stages = woven(stages_of(outw_rings))
    merged = []
    for i, stage in enumerate(early):
        merged.append(stage)
        if i % (2 * SPLIT) == 2 * SPLIT - 1 and outw_stages:
            merged.append(outw_stages.pop(0))
    early[:] = merged + outw_stages
    serve(1)


    lane = lax.broadcasted_iota(jnp.int32, (rows, 128), 1)
    sides = [(lane < HEAD_DIM), (lane >= HEAD_DIM)]
    masks = [side.astype(jnp.float32).astype(jnp.bfloat16) for side in sides]

    def block_back(block):
        context_grad = right_product(rround[block], outw_ref[...]).astype(jnp.bfloat16)
        visible = allow_ref[block] > 0.5
        cuts = [slice(pair * 128, (pair + 1) * 128) for pair in range(band // 128)]
        heads = [(cut, mask) for cut in cuts for mask in masks]
        keys = {cut.start: k_ref[block, :, cut] for cut in cuts}
        scores = [
            right_product(q_ref[block, :, cut] * mask, keys[cut.start]) * scale_factor
            for cut, mask in heads
        ]
        prob_grads = [
            right_product(context_grad[:, cut] * mask, v_ref[block, :, cut]) for cut, mask in heads
        ]
        totals = [
            jnp.sum(jnp.where(visible, jnp.exp(score), 0.0), axis=-1, keepdims=True) for score in scores
        ]
        probs = [
            jnp.where(visible, jnp.exp(score - jnp.log(total)), 0.0)
            for score, total in zip(scores, totals)
        ]
        rounded = [prob.astype(jnp.bfloat16) for prob in probs]
        deltas = [
            jnp.sum(prob * grad, axis=-1, keepdims=True) for prob, grad in zip(probs, prob_grads)
        ]
        score_grads = [
            (prob * (grad - delta) * scale_factor).astype(jnp.bfloat16)
            for prob, grad, delta in zip(probs, prob_grads, deltas)
        ]
        groups = [
            [product(sg, keys[cut.start]) for sg, (cut, _) in zip(score_grads, heads)],
            [left_product(sg, q_ref[block, :, cut]) for sg, (cut, _) in zip(score_grads, heads)],
            [left_product(pr, context_grad[:, cut]) for pr, (cut, _) in zip(rounded, heads)],
        ]
        for j, group in enumerate(groups):
            for pair in range(band // 128):
                grad = jnp.where(sides[0], group[2 * pair], group[2 * pair + 1])
                start = j * band + pair * 128
                qkvg[block, :, start : start + 128] = grad.astype(jnp.bfloat16)
                if j != 1:
                    bias[:, start : start + 128] += jnp.sum(
                        grad.reshape(rows // 8, 8, 128), axis=0
                    )
        serve(PAIR_SERVE)
        fpart[block] = right_product(qkvg[block], qkvw_ref[...]).astype(jnp.bfloat16)

    for load in loads[5:]:
        load.wait()
    for k in range(half):
        block_back(2 * where.order[k] + 1 - where.core)
        first_sum.send(k)
        serve(1)
    for k in range(half):
        block_back(2 * where.order[k] + where.core)
        if k < half - 1:
            first_sum.reduce(k)
        serve(1)

    @pl.loop(0, size)
    def _(t):
        grad = left_product(flat(first_ref[:, :, lanes(t * band, band)]), flat(qkvg[...]))
        qkvwg[t] = grad.astype(jnp.bfloat16).reshape(ring, slab, 3 * band)

    launch(qkv_rings)
    serve(2)
    first_sum.arrive()

    def norm_one(part):
        normed, inv_std = row_stats(hid_ref[part].astype(jnp.float32))
        upper = first_sum.tile(part)
        total = rgrad[me, part] + row_back(upper, normed, inv_std, vec_ref[0:1])
        in_out[part] = total.astype(jnp.bfloat16)
        acc[3] += fold(upper * normed)
        acc[4] += fold(upper)

    tiles(rows, norm_one)
    serve(1)
    down_sum.arrive()

    def finish_hidden(part):
        total = resid_ref[me, part] + down_sum.tile(part) + vec_ref[2:3]
        hidden_out[part] = total.astype(jnp.bfloat16)

    tiles(rows, finish_hidden)
    serve(1)

    span = small.shape[3]

    def put(owner, start, row):
        for t in range(row.shape[1] // 128):
            position = start + t * 128
            small[position // span, owner, :, position % span : position % span + 128] = row[
                :, t * 128 : (t + 1) * 128
            ]

    for i in range(2):
        line = jnp.sum(acc[3 + i], axis=0, keepdims=True)
        for s in range(size):
            put(s, i * band, line[:, s * band : (s + 1) * band])
    start = 2 * band
    line = jnp.sum(bias[...], axis=0, keepdims=True)
    put(me, start, line[:, :band])
    put(me, start + band, line[:, 2 * band :])
    start += 2 * band
    for i in (2, 0, 1):
        put(me, start, jnp.sum(acc[i, :, lanes(me * band, band)], axis=0, keepdims=True))
        start += band
    put(me, start, upb_ref[...])
    start += upb_ref.shape[1]
    put(me, start, vec_ref[3:4, lanes(me * band, band)])
    small_ring.start()

    late = woven(stages_of(qkv_rings + [small_ring]))
    share = max(1, round(len(early) / max(1, len(late)) * LATE_RATE))
    while early or late:
        for _ in range(share):
            if early:
                early.pop(0)()
        for _ in range(LATE_RATE):
            if late:
                late.pop(0)()
    for part in sums + all_rings:
        part.drain()


def back(size, ring, arrays, small_count):
    dma = pltpu.SemaphoreType.DMA
    (act, pre, grads, vec, upb) = arrays[:5]
    moved = arrays[5:]
    rows, width = moved[4].shape
    band = moved[5].shape[2]
    slab = band // ring
    half = size // 2
    ff_band = act.shape[1]
    b16, f32 = jnp.bfloat16, jnp.float32
    vm = pltpu.VMEM
    scratch = [vm(array.shape, array.dtype) for array in moved]
    scratch += [
        vm((size, rows, width), b16),
        vm((size, rows, width), b16),
        vm((ring, ff_band // ring, width), b16),
        vm((size, ring, slab, ff_band), b16),
        dma((len(moved),)),
    ]
    scratch += [vm((half, rows, width), b16)] * 9
    scratch += [
        vm((size, rows, width), b16),
        vm((size, rows, width), b16),
        vm((size, rows, width), f32),
        vm((size, rows, width), b16),
        vm((size, rows, 3 * band), b16),
        vm((ring, slab, width), b16),
        vm((size, ring, slab, 3 * band), b16),
        vm((ring, size, 1, small_count // ring), f32),
        vm((5, 8, width), f32),
        vm((8, 3 * band), f32),
        vm((ring - 1, ff_band // ring, width), b16),
        vm((ring - 1, slab, width), b16),
        vm((ring - 1, size, slab, ff_band), b16),
        vm((ring - 1, size, slab, 3 * band), b16),
        vm((ring - 1, size, 1, small_count // ring), f32),
        vm((size, slab, ff_band), b16),
        vm((size, slab, 3 * band), b16),
        vm((size, 1, small_count // ring), f32),
    ]
    scratch += [dma((3, half))] * 4 + [dma((size,))] * 2 + [dma((8, ring))] * 4 + [dma((8, size))] * 2
    shape = jax.ShapeDtypeStruct
    outs = (
        shape((rows, width), b16),
        shape((rows, width), b16),
        shape((ring, ff_band // ring, width), b16),
        shape((ring, slab, width), b16),
        shape((ring, slab, size * ff_band), b16),
        shape((ring, slab, 3 * width), b16),
        shape((1, small_count), f32),
    )
    return pl.pallas_call(
        functools.partial(back_kernel, size, ring),
        out_shape=outs,
        in_specs=vmem_specs(5) + [pl.BlockSpec(memory_space=pl.ANY)] * len(moved),
        out_specs=tuple(vmem_specs(len(outs))),
        scratch_shapes=scratch,
        compiler_params=pltpu.CompilerParams(
            collective_id=2, has_side_effects=True, vmem_limit_bytes=VMEM_LIMIT
        ),
    )(*arrays)


def fused(
    ring,
    size,
    hidden_in,
    out_grad,
    lengths,
    norm1_gain,
    norm1_bias,
    qkv_weight,
    query_bias,
    value_bias,
    out_weight,
    out_bias,
    norm2_gain,
    norm2_bias,
    up_weight,
    up_bias,
    down_weight,
    down_bias,
):
    rows, width = hidden_in.shape
    band = width // size
    seqs = lengths.shape[1]
    ff_band = up_weight.shape[1] // size
    params = layer_rows(
        (
            norm1_gain, norm1_bias, out_bias, norm2_gain, norm2_bias, down_bias,
            jnp.pad(lengths[0].astype(jnp.bfloat16), (0, band - seqs)),
        ),
        8,
    )
    hidden_all, upstream_all, params_all, qkv_all, up_all = entry(
        size, hidden_in, out_grad, params, qkv_weight, up_weight
    )
    hidden_all = hidden_all.reshape(size * rows, width)
    grad_all = upstream_all.reshape(size * rows, width)
    qkv_cols = qkv_all.reshape(width, 3 * band)
    up_cols = up_all.reshape(width, ff_band)
    gain_one, bias_one, outb_full, gain_two, bias_two, downb_full = (
        params_all[:, i, :band].reshape(width) for i in range(6)
    )
    inputs_wide = hidden_all.astype(jnp.float32)
    first_out, _, _ = layer_norm(inputs_wide, gain_one, bias_one)
    first_in = first_out.astype(jnp.bfloat16)
    projected = product(first_in, qkv_cols)
    by_block = lambda array: array.reshape(size, rows, array.shape[-1])
    queries, key_rows, values, allow, context, attend_part = attend(
        seqs, by_block(projected), params_all, query_bias, value_bias, out_weight
    )
    (attended,) = group_sum(size, [attend_part], (True,), 1)
    residual = (
        inputs_wide
        + attended.reshape(size * rows, width).astype(jnp.float32)
        + outb_full.astype(jnp.float32)
    )
    second_out, _, _ = layer_norm(residual, gain_two, bias_two)
    second_in = second_out.astype(jnp.bfloat16)
    pre_act = product(second_in, up_cols) + up_bias.astype(jnp.float32)
    activ_value, gelu_slope = gelu_parts(pre_act)
    activated = activ_value.astype(jnp.bfloat16)
    upstream = grad_all.astype(jnp.float32)
    pre_grad = right_product(grad_all, down_weight) * gelu_slope
    pre_round = pre_grad.astype(jnp.bfloat16)
    vectors = layer_rows(
        (
            gain_one.astype(jnp.float32),
            gain_two.astype(jnp.float32),
            downb_full.astype(jnp.float32),
            jnp.sum(upstream, axis=0),
        ),
        8,
    )
    slab = band // ring
    lengths_out = (band, band, band, band, band, band, band, ff_band, band)
    hidden_out, in_grad, down_all, outw_all, up_total, qkv_total, small_all = back(
        size,
        ring,
        (
            activated,
            pre_round,
            by_block(grad_all),
            vectors,
            jnp.sum(pre_grad, axis=0)[None],
            second_in,
            up_cols,
            down_weight,
            by_block(residual),
            hidden_in,
            queries,
            key_rows,
            values,
            allow,
            context,
            out_weight,
            by_block(first_in),
            qkv_cols,
        ),
        sum(lengths_out),
    )
    final = lambda array, like: array.reshape(like.shape).astype(jnp.float32)
    flat = small_all.reshape(-1)
    pieces = []
    offset = 0
    for length in lengths_out:
        pieces.append(flat[offset : offset + length])
        offset += length
    gain1_t, bias1_t, qbias_t, vbias_t, outb_t, gain2_t, bias2_t, upb_t, downb_t = pieces
    return (
        hidden_out,
        in_grad,
        gain1_t,
        bias1_t,
        final(qkv_total, qkv_weight),
        qbias_t,
        vbias_t,
        final(outw_all, out_weight),
        outb_t,
        gain2_t,
        bias2_t,
        final(up_total, up_weight),
        upb_t,
        final(down_all, down_weight),
        downb_t,
    )


def layer_rows(vectors, count):
    place = lax.broadcasted_iota(jnp.int32, (count, vectors[0].shape[0]), 0)
    rows = jnp.zeros(place.shape, vectors[0].dtype)
    for i, vector in enumerate(vectors):
        rows = jnp.where(place == i, vector[None], rows)
    return rows


def attend_kernel(seqs, proj_ref, par_ref, qbias_ref, vbias_ref, outw_ref,
                  q_out, k_out, v_out, allow_out, ctx_out, part_out):
    rows, band = q_out.shape[1:]
    lane = lax.broadcasted_iota(jnp.int32, (rows, 128), 1)
    sides = [(lane < HEAD_DIM), (lane >= HEAD_DIM)]
    masks = [side.astype(jnp.float32).astype(jnp.bfloat16) for side in sides]
    above = lax.broadcasted_iota(jnp.int32, (rows, rows), 0).astype(jnp.float32)
    across = lax.broadcasted_iota(jnp.int32, (rows, rows), 1).astype(jnp.float32)

    @pl.loop(0, q_out.shape[0])
    def _(block):
        line = par_ref[block].astype(jnp.float32)[6:7]
        apart = jnp.where(across <= above, 0.0, 1.0)
        end = jnp.zeros((1, 1), jnp.float32)
        for m in range(seqs):
            end = end + line[:, m : m + 1]
            apart = apart + jnp.where(above >= end, 1.0, 0.0) - jnp.where(across >= end, 1.0, 0.0)
        visible = (across <= above) & (apart < 0.5)
        allow_out[block] = jnp.where(visible, 1.0, 0.0)
        queries = (proj_ref[block, :, :band] + qbias_ref[...].astype(jnp.float32)).astype(jnp.bfloat16)
        key_rows = proj_ref[block, :, band : 2 * band].astype(jnp.bfloat16)
        values = (proj_ref[block, :, 2 * band :] + vbias_ref[...].astype(jnp.float32)).astype(
            jnp.bfloat16
        )
        q_out[block] = queries
        k_out[block] = key_rows
        v_out[block] = values
        cuts = [slice(pair * 128, (pair + 1) * 128) for pair in range(band // 128)]
        scores = [
            right_product(queries[:, cut] * mask, key_rows[:, cut]) * (1.0 / math.sqrt(HEAD_DIM))
            for cut in cuts
            for mask in masks
        ]
        totals = [
            jnp.sum(jnp.where(visible, jnp.exp(score), 0.0), axis=-1, keepdims=True) for score in scores
        ]
        probs = [
            jnp.where(visible, jnp.exp(score - jnp.log(total)), 0.0).astype(jnp.bfloat16)
            for score, total in zip(scores, totals)
        ]
        for i, cut in enumerate(cuts):
            value = values[:, cut]
            ctx_out[block, :, cut] = jnp.where(
                sides[0], product(probs[2 * i], value), product(probs[2 * i + 1], value)
            ).astype(jnp.bfloat16)
        part_out[block] = product(ctx_out[block], outw_ref[...]).astype(jnp.bfloat16)


def attend(seqs, projected, params_all, query_bias, value_bias, out_weight):
    size, rows, wide = projected.shape
    band = wide // 3
    shape = jax.ShapeDtypeStruct
    head = shape((size, rows, band), jnp.bfloat16)
    outs = (
        head,
        head,
        head,
        shape((size, rows, rows), jnp.float32),
        head,
        shape((size, rows, out_weight.shape[1]), jnp.bfloat16),
    )
    return pl.pallas_call(
        functools.partial(attend_kernel, seqs),
        out_shape=outs,
        in_specs=vmem_specs(5),
        out_specs=tuple(vmem_specs(len(outs))),
    )(projected, params_all, query_bias[None], value_bias[None], out_weight)


def choose(ring, size, hidden_in, *rest):
    rows, width = hidden_in.shape
    band = width // size
    aligned = width % size == 0 and band % 256 == 0 and band % (16 * ring) == 0
    body = fused if aligned and rows % 128 == 0 and size % 2 == 0 and ring % 4 == 0 else local
    return body(ring, size, hidden_in, *rest)


def solution(mesh):
    in_specs = (
        P(("replica", "shard"), None),
        P(("replica", "shard"), None),
        P(("replica", "shard"), None),
        P("shard"),
        P("shard"),
        P("shard", None),
        P("shard"),
        P("shard"),
        P("shard", None),
        P("shard"),
        P("shard"),
        P("shard"),
        P("shard", None),
        P("shard"),
        P("shard", None),
        P("shard"),
    )
    out_specs = (
        P(("replica", "shard"), None),
        P(("replica", "shard"), None),
        P("shard"),
        P("shard"),
        P("shard", None),
        P("shard"),
        P("shard"),
        P("shard", None),
        P("shard"),
        P("shard"),
        P("shard"),
        P("shard", None),
        P("shard"),
        P("shard", None),
        P("shard"),
    )
    body = functools.partial(choose, mesh.shape["replica"], mesh.shape["shard"])
    return jax.shard_map(body, mesh=mesh, in_specs=in_specs, out_specs=out_specs, check_vma=False)
```
